32 devices in a mesh: ctx: 2 (over y), head: 4 (over x, core), video: 4 (over z).
Axes of the slice: x: 2, y: 2, z: 4, core: 2. Of those that a mesh axis runs over, the one named last changes fastest.
Arguments:
- attention_qkv: bfloat16 [3, 4, 256, 3072], P(None, 'video', 'ctx', 'head'), may hold values from -8 to 8
- inner_qkv: bfloat16 [3, 4, 256, 3072], P(None, 'video', 'ctx', 'head'), may hold values from -3 to 3
- learn_rate: float32 [4, 48, 256], P('video', 'head', 'ctx'), may hold values from 0.001 to 0.01
- segment_id: int32 [4, 256], P('video'), may hold values from 0 to 3, never falling along the last dimension, each value on 1 to 128 neighbouring positions
- video_length: int32 [4], P('video'), may hold values from 128 to 256, as said below
- gate_alpha: float32 [3072], P('head'), may hold values from -1.5 to 1.5
- inner_gain: float32 [48, 64], P('head'), may hold values from 0.5 to 1.5
- inner_shift: float32 [48, 64], P('head'), may hold values from -3 to 3
- first_weight: bfloat16 [48, 64, 256], P('head'), may hold values from -0.75 to 0.75
- first_bias: float32 [48, 256], P('head'), may hold values from -3 to 3
- second_weight: bfloat16 [48, 256, 64], P('head'), may hold values from -0.375 to 0.375
- second_bias: float32 [48, 64], P('head'), may hold values from -3 to 3
- out_weight: bfloat16 [3072, 3072], P('head', 'video'), may hold values from -0.109375 to 0.109375
Outputs:
- mixed: bfloat16 [4, 256, 3072], P('video', 'ctx', 'head')
The draws below stay inside these ranges and needn't reach their ends.
Inputs may be any that keep to these rules, and one draw needn't show every extreme that they name: `segment_id`: segment numbers never fall along a video; each segment holds 1 to 128 positions and some segment exactly 128. `video_length`: some video is live in all 256 positions.
All inputs are finite; a program needn't handle non-finite values.
Results may differ from the reference program's by a relative error of at most 0.017.
Values may be sent and summed in bfloat16 or wider, within the bound.
A program may use at most 64 MiB of HBM per device.

```python
import math
import jax
import jax.numpy as jnp
import numpy as np
from jax import lax

HEADS = 48
HD = 64
D = 3072
INNER = 256
MB = 64
TOK_DEV = 128
SEQ = 256
VIDEOS = 4
N_CTX = 2
N_HEAD = 4


def draw_attention_qkv(key, part):
    base_draw = jnp.clip(jax.random.normal(key, (3, VIDEOS, SEQ, D), jnp.float32), -4.0, 4.0)
    return base_draw.astype(jnp.bfloat16)


def draw_video_length(key, part):
    drawn_len = jax.random.randint(key, (VIDEOS,), SEQ // 2, SEQ + 1)
    longest = jax.random.randint(jax.random.fold_in(key, 5), (), 0, VIDEOS)
    return jnp.where(jnp.arange(VIDEOS) == longest, SEQ, drawn_len).astype(jnp.int32)


def level_of(rng, extent, shards, low, largest):
    factor_of, own = 1.0, jax.random.fold_in(rng, 6)
    for axis_at, parts in shards:
        heights = jnp.exp(jax.random.uniform(jax.random.fold_in(own, axis_at), (parts,), jnp.float32, low / len(shards), largest / len(shards)))
        factor_of = factor_of * jnp.repeat(heights, extent[axis_at] // parts).reshape([-1 if axis == axis_at else 1 for axis in range(len(extent))])
    return factor_of


def profile(count, total, bound, slope):
    loads = [(1 << 20) // math.isqrt(rank ** slope) + 1 for rank in range(2, count + 1)]
    surplus, counts = total - bound - (count - 1), [1] * (count - 1)
    while surplus > 0:
        candidates = [i for i in range(count - 1) if counts[i] < bound]
        mass, remaining = sum([loads[i] for i in candidates]), surplus
        for i in candidates:
            extra = min(bound - counts[i], max(1, remaining * loads[i] // mass), surplus)
            counts[i] = counts[i] + extra
            surplus = surplus - extra
    return np.array([bound] + counts)


def ragged(stream_key, count, total, limit, lean):
    if count == 2:
        one = jax.random.randint(stream_key, (), max(1, total - limit), min(limit, total - 1) + 1)
        return jnp.stack([one, total - one])
    lengths = jnp.asarray(profile(count, total, limit, lean), jnp.int32)
    twos = (count - 1) // 2
    donor, taker = lengths[1:1 + 2 * twos:2], lengths[2:2 + 2 * twos:2]
    slack = jnp.minimum(donor - 1, limit - taker)
    passed = jax.random.randint(jax.random.fold_in(stream_key, 1), (twos,), 0, 1 << 20) % (slack + 1)
    lengths = lengths.at[1:1 + 2 * twos:2].set(donor - passed).at[2:2 + 2 * twos:2].set(taker + passed)
    return lengths[jax.random.permutation(jax.random.fold_in(stream_key, 2), count)]


def noise(key, extent, scale, limit, shards=(), kind=jnp.bfloat16):
    level = level_of(key, extent, shards, -0.22, 0.18) if shards else 1.0
    values = jax.random.normal(key, extent, jnp.float32) * scale * level
    return jnp.minimum(jnp.maximum(values, -limit), limit).astype(kind)


def setup_inputs(seed: int = 0) -> dict:
    streams_of = jax.random.split(jax.random.key(seed), 14)
    attention_qkv = draw_attention_qkv(jax.random.fold_in(streams_of[13], 71), 0)
    inner_qkv = noise(streams_of[1], (3, VIDEOS, SEQ, D), 0.5, 3.0, ((1, 4), (2, 2), (3, 4)))
    learn_rate = jnp.clip(jnp.exp(math.log(0.01) - 2.30258502 * jax.random.uniform(streams_of[2], (VIDEOS, HEADS, SEQ), jnp.float32) ** level_of(streams_of[2], (VIDEOS, HEADS, SEQ), ((0, 4), (1, 4), (2, 2)), -0.2, 0.2)), 0.001, 0.01)
    segment_id = jax.vmap(lambda own: jnp.searchsorted(jnp.cumsum(ragged(own, 2 * N_CTX, SEQ, TOK_DEV, 0)), jnp.arange(SEQ), side="right"))(jax.random.split(streams_of[3], VIDEOS)).reshape((VIDEOS, SEQ)).astype(jnp.int32)
    video_length = draw_video_length(jax.random.fold_in(streams_of[13], 71), 0)
    gate_alpha = jnp.clip(jax.random.uniform(streams_of[5], (D,), jnp.float32, -1.5, 1.5) * level_of(streams_of[5], (D,), ((0, 4),), -0.4, 0.0), -1.5, 1.5)
    inner_gain = jnp.clip(1.0 + 0.1 * jax.random.normal(streams_of[6], (HEADS, HD), jnp.float32), 0.5, 1.5)
    inner_shift = noise(streams_of[7], (HEADS, HD), 0.5, 3.0, ((0, 4),), jnp.float32)
    first_weight = noise(streams_of[8], (HEADS, HD, INNER), HD ** -0.5, 0.75, ((0, 4),))
    first_bias = noise(streams_of[9], (HEADS, INNER), 0.5, 3.0, ((0, 4),), jnp.float32)
    second_weight = noise(streams_of[10], (HEADS, INNER, HD), INNER ** -0.5, 0.375, ((0, 4),))
    second_bias = noise(streams_of[11], (HEADS, HD), 0.5, 3.0, ((0, 4),), jnp.float32)
    out_weight = noise(streams_of[12], (D, D), D ** -0.5, 0.109375, ((0, 4), (1, 4)))
    return dict(attention_qkv=attention_qkv, inner_qkv=inner_qkv, learn_rate=learn_rate, segment_id=segment_id, video_length=video_length, gate_alpha=gate_alpha, inner_gain=inner_gain, inner_shift=inner_shift, first_weight=first_weight, first_bias=first_bias, second_weight=second_weight, second_bias=second_bias, out_weight=out_weight)


gelu_scale = 0.7978845608028654
gelu_cubic = 0.044715

def matmul_high(first_op, second_op):
    return jnp.matmul(first_op, second_op, precision=lax.Precision.HIGHEST)

def gelu_pair(entries):
    inner_arg = gelu_scale * (entries + gelu_cubic * entries * entries * entries)
    tanh_val = jnp.tanh(inner_arg)
    act_val = 0.5 * entries * (1.0 + tanh_val)
    slope_val = 0.5 * (1.0 + tanh_val) + 0.5 * entries * (1.0 - tanh_val * tanh_val) * gelu_scale * (1.0 + 3.0 * gelu_cubic * entries * entries)
    return (act_val, slope_val)

def layer_stats(summed):
    center = summed - lax.optimization_barrier(jnp.mean(summed, axis=-1, keepdims=True))
    variance = lax.optimization_barrier(jnp.mean(center * center, axis=-1, keepdims=True))
    inv_std = lax.rsqrt(variance + 1e-06)
    return (center * inv_std, inv_std)

def lower_mask(row_count):
    row_ids = lax.broadcasted_iota(jnp.int32, (row_count, row_count), 0)
    col_ids = lax.broadcasted_iota(jnp.int32, (row_count, row_count), 1)
    return (row_ids >= col_ids).astype(jnp.float32)

def inner_update(inner_state, key_mb, value_mb, rate_mb, norm_gain, norm_shift):
    weight_one, bias_one, weight_two, bias_two = inner_state
    hidden_pre = matmul_high(key_mb, weight_one) + bias_one
    hidden_act, hidden_slope = gelu_pair(hidden_pre)
    output_pre = matmul_high(hidden_act, weight_two) + bias_two
    normed, inv_std = layer_stats(output_pre)
    residual_err = norm_gain * normed + norm_shift - (value_mb - key_mb)
    scaled_err = residual_err * norm_gain
    grad_two = inv_std * (scaled_err - lax.optimization_barrier(jnp.mean(scaled_err, axis=-1, keepdims=True)) - normed * lax.optimization_barrier(jnp.mean(scaled_err * normed, axis=-1, keepdims=True)))
    grad_one = matmul_high(grad_two, weight_two.T) * hidden_slope
    grad_one = grad_one * rate_mb[:, None]
    grad_two = grad_two * rate_mb[:, None]
    new_state = (weight_one - matmul_high(key_mb.T, grad_one), bias_one - lax.optimization_barrier(jnp.sum(grad_one, axis=0)), weight_two - matmul_high(hidden_act.T, grad_two), bias_two - lax.optimization_barrier(jnp.sum(grad_two, axis=0)))
    return ((grad_one, hidden_act, grad_two), new_state)

def query_side(inner_state, query_mb, key_mb, grad_pack, norm_gain, norm_shift):
    weight_one, bias_one, weight_two, bias_two = inner_state
    grad_one, hidden_act, grad_two = grad_pack
    causal = lower_mask(query_mb.shape[0])
    first_kernel = (matmul_high(query_mb, key_mb.T) + 1.0) * causal
    query_pre = matmul_high(query_mb, weight_one) + bias_one - matmul_high(first_kernel, grad_one)
    query_act, unused_slope = gelu_pair(query_pre)
    second_kernel = (matmul_high(query_act, hidden_act.T) + 1.0) * causal
    query_out = matmul_high(query_act, weight_two) + bias_two - matmul_high(second_kernel, grad_two)
    normed, unused_inv = layer_stats(query_out)
    return query_mb + norm_gain * normed + norm_shift

def head_chain(inner_state, queries, key_rows, values, rate_vals, norm_gain, norm_shift):

    def stepper(loop_state, inputs):
        query_mb, key_mb, value_mb, rate_mb = inputs
        grad_pack, new_state = inner_update(loop_state, key_mb, value_mb, rate_mb, norm_gain, norm_shift)
        return (new_state, query_side(loop_state, query_mb, key_mb, grad_pack, norm_gain, norm_shift))
    final_state, outputs = lax.scan(stepper, inner_state, (queries, key_rows, values, rate_vals))
    return outputs

def attend_block(query_blk, key_ext, value_ext, allowed):
    query_float = query_blk.astype(jnp.float32)
    key_float = key_ext.astype(jnp.float32)
    value_float = value_ext.astype(jnp.float32)
    scores = jnp.einsum('qhd,khd->hqk', query_float, key_float) * HD ** (-0.5)
    scores = jnp.where(allowed[None], scores, -1e+30)
    row_max = lax.optimization_barrier(jnp.max(scores, axis=-1, keepdims=True))
    exp_scores = jnp.exp(scores - row_max)
    soft_weights = (exp_scores / lax.optimization_barrier(jnp.sum(exp_scores, axis=-1, keepdims=True))).astype(jnp.bfloat16)
    soft_float = lax.optimization_barrier(soft_weights).astype(jnp.float32)
    return jnp.einsum('hqk,khd->qhd', soft_float, value_float)

def video_attention(attention_video, segment_row, length_val):
    pad_rows = jnp.zeros((TOK_DEV, D), attention_video.dtype)
    key_pad = jnp.concatenate([pad_rows, attention_video[1], pad_rows], axis=0)
    value_pad = jnp.concatenate([pad_rows, attention_video[2], pad_rows], axis=0)
    fill_ids = jnp.full((TOK_DEV,), -1, jnp.int32)
    seg_pad = jnp.concatenate([fill_ids, segment_row.astype(jnp.int32), fill_ids])

    def one_block(block_index):
        start_row = (block_index * TOK_DEV).astype(jnp.int32)
        query_blk = lax.dynamic_slice_in_dim(attention_video[0], start_row, TOK_DEV, 0).reshape(TOK_DEV, HEADS, HD)
        key_ext = lax.dynamic_slice_in_dim(key_pad, start_row, 3 * TOK_DEV, 0).reshape(3 * TOK_DEV, HEADS, HD)
        value_ext = lax.dynamic_slice_in_dim(value_pad, start_row, 3 * TOK_DEV, 0).reshape(3 * TOK_DEV, HEADS, HD)
        key_seg = lax.dynamic_slice_in_dim(seg_pad, start_row, 3 * TOK_DEV, 0)
        query_seg = lax.dynamic_slice_in_dim(segment_row.astype(jnp.int32), start_row, TOK_DEV, 0)
        query_pos = start_row + jnp.arange(TOK_DEV, dtype=jnp.int32)
        key_pos = start_row - TOK_DEV + jnp.arange(3 * TOK_DEV, dtype=jnp.int32)
        allowed = (key_seg[None, :] == query_seg[:, None]) & ((key_pos[None, :] < length_val) | (key_pos[None, :] == query_pos[:, None]))
        return attend_block(query_blk, key_ext, value_ext, allowed).reshape(TOK_DEV, D)
    blocks = lax.map(one_block, jnp.arange(N_CTX, dtype=jnp.int32))
    return blocks.reshape(SEQ, D)

def reference(attention_qkv, inner_qkv, learn_rate, segment_id, video_length, gate_alpha, inner_gain, inner_shift, first_weight, first_bias, second_weight, second_bias, out_weight):
    positions = jnp.arange(SEQ, dtype=jnp.int32)
    live_rows = (positions[None, :] < video_length[:, None]).astype(jnp.float32)
    attended = jnp.stack([video_attention(attention_qkv[:, video_idx], segment_id[video_idx], video_length[video_idx]) for video_idx in range(VIDEOS)])
    qkv_heads = inner_qkv.astype(jnp.float32).reshape(3, VIDEOS, SEQ, HEADS, HD).transpose(0, 1, 3, 2, 4).reshape(3, VIDEOS, HEADS, SEQ // MB, MB, HD)
    rate_vals = (learn_rate * live_rows[:, None, :]).reshape(VIDEOS, HEADS, SEQ // MB, MB)
    init_state = (first_weight.astype(jnp.float32), first_bias, second_weight.astype(jnp.float32), second_bias)
    per_head = jax.vmap(head_chain)
    per_video = jax.vmap(per_head, in_axes=(None, 0, 0, 0, 0, None, None))
    inner_out = per_video(init_state, qkv_heads[0], qkv_heads[1], qkv_heads[2], rate_vals, inner_gain, inner_shift)
    inner_flat = inner_out.reshape(VIDEOS, HEADS, SEQ, HD).transpose(0, 2, 1, 3).reshape(VIDEOS, SEQ, D)
    combined = ((attended + jnp.tanh(gate_alpha) * inner_flat) * live_rows[:, :, None]).astype(jnp.bfloat16)
    flat_rows = combined.reshape(VIDEOS * SEQ, D)
    block_width = D // N_HEAD
    mixed_sum = jnp.zeros((VIDEOS * SEQ, D), jnp.float32)
    for block_idx in range(N_HEAD):
        lower_col = block_idx * block_width
        partial_prod = jnp.dot(flat_rows[:, lower_col:lower_col + block_width], out_weight[lower_col:lower_col + block_width], preferred_element_type=jnp.float32)
        rounded_part = lax.optimization_barrier(partial_prod.astype(jnp.bfloat16)).astype(jnp.float32)
        mixed_sum = mixed_sum + rounded_part
    return mixed_sum.astype(jnp.bfloat16).reshape(VIDEOS, SEQ, D)
```

```python
from functools import partial

import jax
import jax.numpy as jnp
from jax import lax
from jax.experimental import pallas as pl
from jax.experimental.pallas import tpu as pltpu
from jax.sharding import PartitionSpec as P

HD = 64
MB = 64


gelu_scale = 0.7978845608028654
gelu_cubic = 0.044715


def with_halo(cells, sides, width):
    for axis, dim in sides:
        count = lax.axis_size(axis)
        ends = count - 1
        head = lax.slice_in_dim(cells, 0, width, axis=dim)
        tail = lax.slice_in_dim(cells, cells.shape[dim] - width, cells.shape[dim], axis=dim)
        cells = jnp.concatenate(
            [
                lax.ppermute(tail, axis, [(i, (i + 1) % count) for i in range(ends)]),
                cells,
                lax.ppermute(head, axis, [((i + 1) % count, i) for i in range(ends)]),
            ],
            axis=dim,
        )
    return cells


def matmul_high(first_op, second_op):
    return jnp.matmul(first_op, second_op, precision=lax.Precision.HIGHEST)


def gelu_pair(entries):
    inner_arg = gelu_scale * (entries + gelu_cubic * entries * entries * entries)
    tanh_val = jnp.tanh(inner_arg)
    act_val = 0.5 * entries * (1.0 + tanh_val)
    slope_val = 0.5 * (1.0 + tanh_val) + 0.5 * entries * (
        1.0 - tanh_val * tanh_val
    ) * gelu_scale * (1.0 + 3.0 * gelu_cubic * entries * entries)
    return (act_val, slope_val)


def layer_stats(summed):
    center = summed - jnp.mean(summed, axis=-1, keepdims=True)
    variance = jnp.mean(center * center, axis=-1, keepdims=True)
    inv_std = lax.rsqrt(variance + 1e-06)
    return (center * inv_std, inv_std)


def lower_mask(row_count):
    row_ids = lax.broadcasted_iota(jnp.int32, (row_count, row_count), 0)
    col_ids = lax.broadcasted_iota(jnp.int32, (row_count, row_count), 1)
    return (row_ids >= col_ids).astype(jnp.float32)


def inner_update(inner_state, key_mb, value_mb, rate_mb, norm_gain, norm_shift):
    weight_one, bias_one, weight_two, bias_two = inner_state
    hidden_pre = matmul_high(key_mb, weight_one) + bias_one
    hidden_act, hidden_slope = gelu_pair(hidden_pre)
    output_pre = matmul_high(hidden_act, weight_two) + bias_two
    normed, inv_std = layer_stats(output_pre)
    residual_err = norm_gain * normed + norm_shift - (value_mb - key_mb)
    scaled_err = residual_err * norm_gain
    grad_two = inv_std * (
        scaled_err
        - jnp.mean(scaled_err, axis=-1, keepdims=True)
        - normed * jnp.mean(scaled_err * normed, axis=-1, keepdims=True)
    )
    grad_one = matmul_high(grad_two, weight_two.T) * hidden_slope
    grad_one = grad_one * rate_mb[:, None]
    grad_two = grad_two * rate_mb[:, None]
    new_state = (
        weight_one - matmul_high(key_mb.T, grad_one),
        bias_one - jnp.sum(grad_one, axis=0),
        weight_two - matmul_high(hidden_act.T, grad_two),
        bias_two - jnp.sum(grad_two, axis=0),
    )
    return ((grad_one, hidden_act, grad_two), new_state)


def query_side(inner_state, query_mb, key_mb, grad_pack, norm_gain, norm_shift):
    weight_one, bias_one, weight_two, bias_two = inner_state
    grad_one, hidden_act, grad_two = grad_pack
    causal = lower_mask(query_mb.shape[0])
    first_kernel = (matmul_high(query_mb, key_mb.T) + 1.0) * causal
    query_pre = matmul_high(query_mb, weight_one) + bias_one - matmul_high(first_kernel, grad_one)
    query_act, unused_slope = gelu_pair(query_pre)
    second_kernel = (matmul_high(query_act, hidden_act.T) + 1.0) * causal
    query_out = matmul_high(query_act, weight_two) + bias_two - matmul_high(second_kernel, grad_two)
    normed, unused_inv = layer_stats(query_out)
    return query_mb + norm_gain * normed + norm_shift


def chain_scan(
    keep_queries, inner_state, queries, key_rows, values, rate_vals, norm_gain, norm_shift
):

    def stepper(loop_state, inputs):
        query_mb, key_mb, value_mb, rate_mb = inputs
        grad_pack, new_state = inner_update(
            loop_state, key_mb, value_mb, rate_mb, norm_gain, norm_shift
        )
        return (
            new_state,
            query_side(loop_state, query_mb, key_mb, grad_pack, norm_gain, norm_shift),
        )

    return lax.scan(stepper, inner_state, (queries, key_rows, values, rate_vals))


def pad_heads(array_in, total_heads, fill_value):
    extra = total_heads - array_in.shape[0]
    filler = jnp.full((extra,) + array_in.shape[1:], fill_value, array_in.dtype)
    return jnp.concatenate([array_in, filler], axis=0)


LANE = 128
MESH_ID = pl.DeviceIdType.MESH


def dot_nn(left, right):
    return lax.dot_general(
        left, right, (((1,), (0,)), ((), ())), preferred_element_type=jnp.float32
    )


def dot_nt(left, right):
    return lax.dot_general(
        left, right, (((1,), (1,)), ((), ())), preferred_element_type=jnp.float32
    )


def dot_tn(left, right):
    return lax.dot_general(
        left, right, (((0,), (0,)), ((), ())), preferred_element_type=jnp.float32
    )


def gelu_only(entries):
    inner_arg = gelu_scale * (entries + gelu_cubic * entries * entries * entries)
    return 0.5 * entries * (1.0 + jnp.tanh(inner_arg))


def half_mean(cells, left):
    first = jnp.sum(jnp.where(left, cells, 0.0), axis=-1, keepdims=True)
    second = jnp.sum(jnp.where(left, 0.0, cells), axis=-1, keepdims=True)
    return jnp.where(left, first, second) * (1.0 / HD)


def half_stats(summed, left):
    center = summed - half_mean(summed, left)
    inv_std = lax.rsqrt(half_mean(center * center, left) + 1e-06)
    return (center * inv_std, inv_std)


def split_heads(cells, left):
    wide = cells.astype(jnp.float32)
    return jnp.concatenate(
        [jnp.where(left, wide, 0.0), jnp.where(left, 0.0, wide)], axis=0
    ).astype(cells.dtype)


def fused_kernel(
    aqkv,
    iqkv,
    rate,
    first_w,
    second_w,
    out_w,
    seg,
    length,
    gate,
    gain,
    shift,
    first_b,
    second_b,
    out,
    a_rows,
    i_rows,
    rates,
    fw,
    sw,
    ow,
    w1m,
    w1b,
    w2m,
    w2b,
    b1,
    b2,
    gain_s,
    shift_s,
    rate_a,
    rate_b,
    bias,
    inner,
    comb,
    gathered,
    parts,
    arrived,
    total,
    load_sem,
    y_send,
    y_recv,
    back_send,
    back_recv,
    z_send,
    z_recv,
    own_sem,
    r_send,
    r_recv,
    t_send,
    t_recv,
):
    slabs, _, seq, _ = a_rows.shape
    tok = aqkv.shape[2]
    hidden = first_b.shape[1]
    count = lax.axis_size("head")
    c = lax.axis_index("ctx")
    h = lax.axis_index("head")
    v = lax.axis_index("video")
    other = 1 - c
    mine = pl.multiple_of(c * tok, tok)
    theirs = pl.multiple_of(other * tok, tok)
    pairs_heads = 2 * slabs

    def columns(owner, slab):
        return pl.ds(pl.multiple_of((owner * slabs + slab) * LANE, LANE), LANE)

    loads = []
    for slab in range(slabs):
        loads.append(
            pltpu.make_async_copy(
                iqkv.at[:, 0, :, columns(c, slab)],
                i_rows.at[slab, :, pl.ds(mine, tok), :],
                load_sem.at[slab],
            )
        )
    loads.append(pltpu.make_async_copy(rate.at[0], rates.at[c], load_sem.at[2 * slabs]))
    loads.append(
        pltpu.make_async_copy(
            first_w.at[pl.ds(c * pairs_heads, pairs_heads)], fw, load_sem.at[2 * slabs + 1]
        )
    )
    loads.append(
        pltpu.make_async_copy(
            second_w.at[pl.ds(c * pairs_heads, pairs_heads)], sw, load_sem.at[2 * slabs + 2]
        )
    )
    a_loads = [
        pltpu.make_async_copy(
            aqkv.at[:, 0, :, columns(c, slab)],
            a_rows.at[slab, :, pl.ds(mine, tok), :],
            load_sem.at[slabs + slab],
        )
        for slab in range(slabs)
    ]
    ow_load = pltpu.make_async_copy(out_w, ow, load_sem.at[2 * slabs + 3])
    for copy in loads + a_loads + [ow_load]:
        copy.start()

    barrier = pltpu.get_barrier_semaphore()
    pl.semaphore_signal(
        barrier, inc=1, device_id={"ctx": other}, device_id_type=MESH_ID
    )
    everyone = count * count
    place = h * count + v
    for step in range(1, everyone):
        peer = lax.rem(place + step, everyone)
        pl.semaphore_signal(
            barrier,
            inc=1,
            device_id={"head": peer // count, "video": lax.rem(peer, count)},
            device_id_type=MESH_ID,
        )
    pl.semaphore_wait(barrier, everyone)

    def to_partner(src, dst, send, recv):
        return pltpu.make_async_remote_copy(
            src_ref=src,
            dst_ref=dst,
            send_sem=send,
            recv_sem=recv,
            device_id={"ctx": other},
            device_id_type=MESH_ID,
        )

    rate_out = to_partner(
        rate.at[0], rates.at[c], y_send.at[2 * slabs], y_recv.at[2 * slabs]
    )
    rate_out.start()
    i_out = [
        to_partner(
            iqkv.at[:, 0, :, columns(other, slab)],
            i_rows.at[slab, :, pl.ds(mine, tok), :],
            y_send.at[slab],
            y_recv.at[slab],
        )
        for slab in range(slabs)
    ]
    a_out = [
        to_partner(
            aqkv.at[:, 0, :, columns(other, slab)],
            a_rows.at[slab, :, pl.ds(mine, tok), :],
            y_send.at[slabs + slab],
            y_recv.at[slabs + slab],
        )
        for slab in range(slabs)
    ]
    for copy in i_out + a_out:
        copy.start()

    seq_ids = lax.broadcasted_iota(jnp.int32, (seq, seq), 1)
    row_ids = lax.broadcasted_iota(jnp.int32, (seq, seq), 0)
    len_val = length[0]
    segs = jnp.broadcast_to(seg[...].astype(jnp.float32), (seq, seq))
    allowed = (segs == segs.T) & ((seq_ids < len_val) | (seq_ids == row_ids))
    bias[...] = jnp.where(allowed, 0.0, -1e30)
    live = (lax.broadcasted_iota(jnp.int32, (seq, LANE), 0) < len_val).astype(jnp.float32)
    left_row = lax.broadcasted_iota(jnp.int32, (1, LANE), 1) < HD
    left = lax.broadcasted_iota(jnp.int32, (MB, LANE), 1) < HD
    left_hidden = lax.broadcasted_iota(jnp.int32, (hidden, LANE), 1) < HD
    left_seq = lax.broadcasted_iota(jnp.int32, (seq, LANE), 1) < HD
    tri = lax.broadcasted_iota(jnp.int32, (MB, MB), 0) >= lax.broadcasted_iota(
        jnp.int32, (MB, MB), 1
    )
    tri = tri.astype(jnp.float32)
    tri_pair = jnp.concatenate([tri, tri], axis=0)

    for copy in loads:
        copy.wait()

    def pair_row(ref, head):
        return jnp.concatenate([ref[pl.ds(head, 1), :], ref[pl.ds(head + 1, 1), :]], axis=1)

    for slab in range(slabs):
        head = c * pairs_heads + 2 * slab
        gain_s[slab] = pair_row(gain, head)
        shift_s[slab] = pair_row(shift, head)
        b1[slab] = pair_row(first_b, head)
        b2[slab] = pair_row(second_b, head)
        w1_a = fw[2 * slab]
        w1_b = fw[2 * slab + 1]
        w1m[slab, 0:HD] = w1_a.astype(jnp.float32)
        w1m[slab, HD:LANE] = w1_b.astype(jnp.float32)
        w1b[slab] = jnp.zeros_like(w1b[slab])
        w1b[slab, 0:HD, 0:hidden] = w1_a
        w1b[slab, HD:LANE, hidden : 2 * hidden] = w1_b
        w2 = jnp.concatenate(
            [sw[2 * slab].astype(jnp.float32), sw[2 * slab + 1].astype(jnp.float32)], axis=1
        )
        w2m[slab] = w2
        w2b[slab, 0:hidden] = jnp.where(left_hidden, w2, 0.0).astype(jnp.bfloat16)
        w2b[slab, hidden : 2 * hidden] = jnp.where(left_hidden, 0.0, w2).astype(jnp.bfloat16)

    rate_out.wait_recv()
    for slab in range(slabs):
        head = c * pairs_heads + 2 * slab
        for part in range(seq // tok):
            rows = slice(part * tok, (part + 1) * tok)
            for ahead, store in ((0, rate_a), (1, rate_b)):
                row = rates[part, pl.ds(head + ahead, 1), :]
                store[slab, rows] = jnp.broadcast_to(row, (LANE, tok)).T * live[rows]

    for copy in i_out:
        copy.wait_recv()

    def inner_step(slab, row):
        rows = pl.ds(row, MB)
        query, key, value = (i_rows[slab, kind, rows, :] for kind in range(3))
        query_f = query.astype(jnp.float32)
        key_f = key.astype(jnp.float32)
        value_f = value.astype(jnp.float32)
        norm_gain = gain_s[slab]
        norm_shift = shift_s[slab]
        weight_one = w1b[slab]
        weight_two = w2b[slab]
        bias_one = b1[slab]
        bias_two = b2[slab]
        pre = dot_nn(jnp.concatenate([key, query], axis=0), weight_one) + bias_one
        hidden_act, slope = gelu_pair(pre[:MB])
        hidden_b = hidden_act.astype(jnp.bfloat16)
        normed, inv_std = half_stats(dot_nn(hidden_b, weight_two) + bias_two, left)
        scaled = (norm_gain * normed + norm_shift - (value_f - key_f)) * norm_gain
        grad_two = inv_std * (
            scaled - half_mean(scaled, left) - normed * half_mean(scaled * normed, left)
        )
        e_a = rate_a[slab, rows, :]
        e_b = rate_b[slab, rows, :]
        wide = [e_a] * (hidden // LANE) + [e_b] * (hidden // LANE)
        grad_one = dot_nt(grad_two.astype(jnp.bfloat16), weight_two) * slope
        grad_one = grad_one * jnp.concatenate(wide, axis=1)
        grad_two = grad_two * jnp.where(left, e_a, e_b)
        one_b = grad_one.astype(jnp.bfloat16)
        two_b = grad_two.astype(jnp.bfloat16)

        first_kernel = (dot_nt(split_heads(query, left), key) + 1.0) * tri_pair
        first_kernel = first_kernel.astype(jnp.bfloat16)
        fix = jnp.concatenate(
            [
                dot_nn(first_kernel[:MB], one_b[:, :hidden]),
                dot_nn(first_kernel[MB:], one_b[:, hidden:]),
            ],
            axis=1,
        )
        query_act = gelu_only(pre[MB:] - fix).astype(jnp.bfloat16)
        second_kernel = jnp.concatenate(
            [
                dot_nt(query_act[:, :hidden], hidden_b[:, :hidden]),
                dot_nt(query_act[:, hidden:], hidden_b[:, hidden:]),
            ],
            axis=0,
        )
        second_kernel = ((second_kernel + 1.0) * tri_pair).astype(jnp.bfloat16)
        fix_two = dot_nn(second_kernel, two_b)
        fix_two = jnp.where(left, fix_two[:MB], fix_two[MB:])
        query_out = dot_nn(query_act, weight_two) + bias_two - fix_two
        normed_out, _ = half_stats(query_out, left)
        inner[slab, rows, :] = query_f + norm_gain * normed_out + norm_shift

        up_one = dot_tn(key, one_b)
        one_first = w1m[slab, 0:HD] - up_one[:HD, :hidden]
        one_second = w1m[slab, HD:LANE] - up_one[HD:, hidden:]
        up_two = dot_tn(hidden_b, two_b)
        two_new = w2m[slab] - jnp.where(left_hidden, up_two[:hidden], up_two[hidden:])
        w1m[slab, 0:HD] = one_first
        w1m[slab, HD:LANE] = one_second
        w1b[slab, 0:HD, 0:hidden] = one_first.astype(jnp.bfloat16)
        w1b[slab, HD:LANE, hidden : 2 * hidden] = one_second.astype(jnp.bfloat16)
        w2m[slab] = two_new
        w2b[slab, 0:hidden] = jnp.where(left_hidden, two_new, 0.0).astype(jnp.bfloat16)
        w2b[slab, hidden : 2 * hidden] = jnp.where(left_hidden, 0.0, two_new).astype(
            jnp.bfloat16
        )
        b1[slab] = bias_one - jnp.sum(grad_one, axis=0, keepdims=True)
        b2[slab] = bias_two - jnp.sum(grad_two, axis=0, keepdims=True)

    def batch_step(batch, carry):
        row = pl.multiple_of(batch * MB, MB)
        for slab in range(slabs):
            inner_step(slab, row)
        return carry

    lax.fori_loop(0, seq // MB, batch_step, 0)

    def to_video(src, video, spot, step):
        return pltpu.make_async_remote_copy(
            src_ref=src,
            dst_ref=gathered.at[v, spot],
            send_sem=z_send.at[spot, step - 1],
            recv_sem=z_recv.at[spot, step - 1],
            device_id={"video": video},
            device_id_type=MESH_ID,
        )

    def spread(src, spot):
        copies = []
        for step in range(1, count):
            copy = to_video(src, lax.rem(v + step, count), spot, step)
            copy.start()
            copies.append(copy)
        return copies

    z_out = []
    backs = []
    owns = []
    for slab in range(slabs):
        a_loads[slab].wait()
        a_out[slab].wait_recv()
        query, key, value = (a_rows[slab, kind] for kind in range(3))
        scores = dot_nt(split_heads(query, left_seq), key) * HD ** (-0.5)
        halves = []
        for part in range(2):
            mine_scores = scores[part * seq : (part + 1) * seq] + bias[...]
            top = jnp.max(mine_scores, axis=-1, keepdims=True)
            weights = jnp.exp(mine_scores - top)
            mass = jnp.sum(weights, axis=-1, keepdims=True)
            halves.append(dot_nn(weights.astype(jnp.bfloat16), value) / mass)
        attended = jnp.where(left_seq, halves[0], halves[1])
        gate_row = jnp.tanh(gate[:, columns(c, slab)])
        comb[slab] = ((attended + gate_row * inner[slab]) * live).astype(jnp.bfloat16)
        spot = c * slabs + slab
        back = to_partner(
            comb.at[slab, pl.ds(theirs, tok), :],
            gathered.at[v, spot],
            back_send.at[slab],
            back_recv.at[slab],
        )
        back.start()
        backs.append(back)
        own = pltpu.make_async_copy(
            comb.at[slab, pl.ds(mine, tok), :], gathered.at[v, spot], own_sem.at[slab]
        )
        own.start()
        owns.append(own)
        z_out += spread(comb.at[slab, pl.ds(mine, tok), :], spot)
        if slab:
            backs[slab - 1].wait_recv()
            far = other * slabs + slab - 1
            z_out += spread(gathered.at[v, far], far)
    backs[slabs - 1].wait_recv()
    far = other * slabs + slabs - 1
    z_out += spread(gathered.at[v, far], far)
    for own in owns:
        own.wait()
    ow_load.wait()

    def owner_of(video):
        return lax.rem(video, 2) * (count // 2) + video // 2

    def video_of(head):
        return lax.rem(head, count // 2) * 2 + head // (count // 2)

    for step in range(1, count):
        source = lax.rem(v + count - step, count)
        for spot in range(2 * slabs):
            pltpu.make_async_remote_copy(
                src_ref=gathered.at[source, spot],
                dst_ref=gathered.at[source, spot],
                send_sem=z_send.at[spot, step - 1],
                recv_sem=z_recv.at[spot, step - 1],
                device_id={"video": source},
                device_id_type=MESH_ID,
            ).wait_recv()
    rows_all = jnp.concatenate(
        [
            jnp.concatenate([gathered[video, spot] for spot in range(2 * slabs)], axis=1)
            for video in range(count)
        ],
        axis=0,
    )
    width = ow.shape[1]
    chunk = 2 * LANE if width % (2 * LANE) == 0 else width
    for start in range(0, width, chunk):
        piece = dot_nn(rows_all, ow[:, start : start + chunk]).astype(jnp.bfloat16)
        for video in range(count):
            parts[video, :, start : start + chunk] = piece[video * tok : (video + 1) * tok]

    r_out = []
    for step in range(count - 1, 0, -1):
        head = lax.rem(h + step, count)
        copy = pltpu.make_async_remote_copy(
            src_ref=parts.at[video_of(head)],
            dst_ref=arrived.at[step - 1],
            send_sem=r_send.at[step - 1],
            recv_sem=r_recv.at[step - 1],
            device_id={"head": head},
            device_id_type=MESH_ID,
        )
        copy.start()
        r_out.append(copy)
    for copy in r_out:
        copy.wait_recv()
    summed = parts[video_of(h)].astype(jnp.float32)
    for step in range(count - 1):
        summed = summed + arrived[step].astype(jnp.float32)
    total[...] = summed.astype(jnp.bfloat16)

    to_head, to_v = v, video_of(h)
    stays = (to_head == h) & (to_v == v)
    final = pltpu.make_async_remote_copy(
        src_ref=total,
        dst_ref=out.at[0],
        send_sem=t_send,
        recv_sem=t_recv,
        device_id={"head": to_head, "video": to_v},
        device_id_type=MESH_ID,
    )

    @pl.when(stays)
    def _():
        out[0] = total[...]

    @pl.when(jnp.logical_not(stays))
    def _():
        final.start()
        final.wait()

    for copy in [rate_out] + i_out + a_out + backs + z_out + r_out:
        copy.wait_send()


def fused_on_device(
    attention_qkv,
    inner_qkv,
    learn_rate,
    segment_id,
    video_length,
    gate_alpha,
    inner_gain,
    inner_shift,
    first_weight,
    first_bias,
    second_weight,
    second_bias,
    out_weight,
):
    tok = attention_qkv.shape[2]
    width_dev = attention_qkv.shape[3]
    count = lax.axis_size("head")
    ctx_count = lax.axis_size("ctx")
    seq = tok * ctx_count
    slabs = width_dev // LANE // ctx_count
    heads = width_dev // HD
    hidden = first_weight.shape[2]
    columns = out_weight.shape[1]
    half = jnp.bfloat16
    full = jnp.float32
    hbm = pl.BlockSpec(memory_space=pl.ANY)
    vmem = pl.BlockSpec(memory_space=pltpu.VMEM)
    smem = pl.BlockSpec(memory_space=pltpu.SMEM)
    dma = pltpu.SemaphoreType.DMA
    return pl.pallas_call(
        fused_kernel,
        out_shape=jax.ShapeDtypeStruct((1, tok, columns), half),
        in_specs=[hbm] * 6 + [vmem, smem] + [vmem] * 5,
        out_specs=vmem,
        scratch_shapes=[
            pltpu.VMEM((slabs, 3, seq, LANE), half),
            pltpu.VMEM((slabs, 3, seq, LANE), half),
            pltpu.VMEM((ctx_count, heads, tok), full),
            pltpu.VMEM((2 * slabs,) + first_weight.shape[1:], half),
            pltpu.VMEM((2 * slabs,) + second_weight.shape[1:], half),
            pltpu.VMEM(out_weight.shape, half),
            pltpu.VMEM((slabs, LANE, hidden), full),
            pltpu.VMEM((slabs, LANE, 2 * hidden), half),
            pltpu.VMEM((slabs, hidden, LANE), full),
            pltpu.VMEM((slabs, 2 * hidden, LANE), half),
            pltpu.VMEM((slabs, 1, 2 * hidden), full),
            pltpu.VMEM((slabs, 1, LANE), full),
            pltpu.VMEM((slabs, 1, LANE), full),
            pltpu.VMEM((slabs, 1, LANE), full),
            pltpu.VMEM((slabs, seq, LANE), full),
            pltpu.VMEM((slabs, seq, LANE), full),
            pltpu.VMEM((seq, seq), full),
            pltpu.VMEM((slabs, seq, LANE), full),
            pltpu.VMEM((slabs, seq, LANE), half),
            pltpu.VMEM((count, 2 * slabs, tok, LANE), half),
            pltpu.VMEM((count, tok, columns), half),
            pltpu.VMEM((count - 1, tok, columns), half),
            pltpu.VMEM((tok, columns), half),
            dma((2 * slabs + 4,)),
            dma((2 * slabs + 1,)),
            dma((2 * slabs + 1,)),
            dma((slabs,)),
            dma((slabs,)),
            dma((2 * slabs, count - 1)),
            dma((2 * slabs, count - 1)),
            dma((slabs,)),
            dma((count - 1,)),
            dma((count - 1,)),
            dma,
            dma,
        ],
        compiler_params=pltpu.CompilerParams(
            collective_id=0, has_side_effects=True, vmem_limit_bytes=60 * 1024 * 1024
        ),
    )(
        attention_qkv,
        inner_qkv,
        learn_rate,
        first_weight,
        second_weight,
        out_weight,
        segment_id,
        video_length,
        gate_alpha[None],
        inner_gain,
        inner_shift,
        first_bias,
        second_bias,
    )


def general_on_device(
    attention_qkv,
    inner_qkv,
    learn_rate,
    segment_id,
    video_length,
    gate_alpha,
    inner_gain,
    inner_shift,
    first_weight,
    first_bias,
    second_weight,
    second_bias,
    out_weight,
):
    tok_count = attention_qkv.shape[2]
    width_dev = attention_qkv.shape[3]
    heads_dev = width_dev // HD
    ctx_index = lax.axis_index("ctx")
    ctx_count = lax.axis_size("ctx")
    positions = ctx_index * tok_count + jnp.arange(tok_count, dtype=jnp.int32)
    length_val = video_length[0]
    live_rows = (positions < length_val).astype(jnp.float32)
    kv_pair = attention_qkv[1:, 0]
    kv_wide = with_halo(kv_pair, (("ctx", 1),), tok_count)
    key_pos = (ctx_index - 1) * tok_count + jnp.arange(3 * tok_count, dtype=jnp.int32)
    seg_row = segment_id[0]
    fill_ids = jnp.full((tok_count,), -1, jnp.int32)
    seg_pad = jnp.concatenate([fill_ids, seg_row, fill_ids])
    key_seg = lax.dynamic_slice_in_dim(seg_pad, ctx_index * tok_count, 3 * tok_count, 0)
    query_seg = lax.dynamic_slice_in_dim(seg_row, ctx_index * tok_count, tok_count, 0)
    allowed = (key_seg[None, :] == query_seg[:, None]) & (
        (key_pos[None, :] < length_val) | (key_pos[None, :] == positions[:, None])
    )
    query_heads = attention_qkv[0, 0].reshape(tok_count, heads_dev, HD)
    key_heads = kv_wide[0].reshape(3 * tok_count, heads_dev, HD)
    value_heads = kv_wide[1].reshape(3 * tok_count, heads_dev, HD)
    scores = jnp.einsum(
        "qhd,khd->hqk", query_heads, key_heads, preferred_element_type=jnp.float32
    ) * HD ** (-0.5)
    scores = jnp.where(allowed[None], scores, -1e30)
    row_max = jnp.max(scores, axis=-1, keepdims=True)
    exp_scores = jnp.exp(scores - row_max)
    soft_weights = (exp_scores / jnp.sum(exp_scores, axis=-1, keepdims=True)).astype(jnp.bfloat16)
    attended = jnp.einsum(
        "hqk,khd->qhd", soft_weights, value_heads, preferred_element_type=jnp.float32
    ).reshape(tok_count, width_dev)
    init_state = (
        first_weight.astype(jnp.float32),
        first_bias,
        second_weight.astype(jnp.float32),
        second_bias,
    )
    rate_rows = learn_rate[0] * live_rows[None, :]
    heads_each = -(-heads_dev // ctx_count)
    heads_padded = heads_each * ctx_count
    rows_heads = inner_qkv[:, 0].reshape(3, tok_count, heads_dev, HD)
    rows_padded = jnp.concatenate(
        [rows_heads, jnp.zeros((3, tok_count, heads_padded - heads_dev, HD), rows_heads.dtype)],
        axis=2,
    )
    rates_padded = pad_heads(rate_rows, heads_padded, 0.0)
    whole_rows = lax.all_to_all(rows_padded, "ctx", split_axis=2, concat_axis=1, tiled=True)
    whole_rates = lax.all_to_all(rates_padded, "ctx", split_axis=0, concat_axis=1, tiled=True)
    seq_count = whole_rows.shape[1]
    full_batches = seq_count // MB
    local_qkv = (
        whole_rows.astype(jnp.float32)
        .transpose(0, 2, 1, 3)
        .reshape(3, heads_each, full_batches, MB, HD)
    )
    local_rates = whole_rates.reshape(heads_each, full_batches, MB)
    first_head = ctx_index * heads_each
    local_gain = lax.dynamic_slice_in_dim(
        pad_heads(inner_gain, heads_padded, 1.0), first_head, heads_each, 0
    )
    local_shift = lax.dynamic_slice_in_dim(
        pad_heads(inner_shift, heads_padded, 0.0), first_head, heads_each, 0
    )
    local_state = tuple(
        (
            lax.dynamic_slice_in_dim(
                pad_heads(piece_arr, heads_padded, 0.0), first_head, heads_each, 0
            )
            for piece_arr in init_state
        )
    )
    unused_final, saved_local = jax.vmap(partial(chain_scan, True))(
        local_state, local_qkv[0], local_qkv[1], local_qkv[2], local_rates, local_gain, local_shift
    )
    out_rows = saved_local.reshape(heads_each, seq_count, HD).transpose(1, 0, 2)
    back_rows = lax.all_to_all(
        out_rows.astype(jnp.bfloat16), "ctx", split_axis=0, concat_axis=1, tiled=True
    ).astype(out_rows.dtype)
    inner_flat = back_rows[:, :heads_dev].reshape(tok_count, width_dev)
    combined = ((attended + jnp.tanh(gate_alpha) * inner_flat) * live_rows[:, None]).astype(
        jnp.bfloat16
    )
    terms = jnp.dot(
        combined,
        lax.all_gather(out_weight, "video", axis=1, tiled=True),
        preferred_element_type=jnp.float32,
    )
    mixed = lax.psum_scatter(terms.astype(jnp.bfloat16), "head", scatter_dimension=1, tiled=True)
    return mixed[None]


def solution(mesh):
    placed = (
        P(None, "video", "ctx", "head"),
        P(None, "video", "ctx", "head"),
        P("video", "head", "ctx"),
        P("video", None),
        P("video"),
        P("head"),
        P("head", None),
        P("head", None),
        P("head", None, None),
        P("head", None),
        P("head", None, None),
        P("head", None),
        P("head", "video"),
    )
    shape = mesh.shape
    fused = shape["ctx"] == 2 and shape["head"] == shape["video"] and shape["head"] % 2 == 0

    def on_device(*args):
        heads_dev = args[0].shape[3] // HD
        if fused and heads_dev % (2 * shape["ctx"]) == 0 and args[0].shape[2] % 128 == 0:
            return fused_on_device(*args)
        return general_on_device(*args)

    return jax.shard_map(
        on_device, mesh=mesh, in_specs=placed, out_specs=P("video", "ctx", "head"), check_vma=False
    )
```

```python
from functools import partial

import jax
import jax.numpy as jnp
from jax import lax
from jax.experimental import pallas as pl
from jax.experimental.pallas import tpu as pltpu
from jax.sharding import PartitionSpec as P

HD = 64
MB = 64


gelu_scale = 0.7978845608028654
gelu_cubic = 0.044715


def with_halo(cells, sides, width):
    for axis, dim in sides:
        count = lax.axis_size(axis)
        ends = count - 1
        head = lax.slice_in_dim(cells, 0, width, axis=dim)
        tail = lax.slice_in_dim(cells, cells.shape[dim] - width, cells.shape[dim], axis=dim)
        cells = jnp.concatenate(
            [
                lax.ppermute(tail, axis, [(i, (i + 1) % count) for i in range(ends)]),
                cells,
                lax.ppermute(head, axis, [((i + 1) % count, i) for i in range(ends)]),
            ],
            axis=dim,
        )
    return cells


def matmul_high(first_op, second_op):
    return jnp.matmul(first_op, second_op, precision=lax.Precision.HIGHEST)


def gelu_pair(entries):
    inner_arg = gelu_scale * (entries + gelu_cubic * entries * entries * entries)
    tanh_val = jnp.tanh(inner_arg)
    act_val = 0.5 * entries * (1.0 + tanh_val)
    slope_val = 0.5 * (1.0 + tanh_val) + 0.5 * entries * (
        1.0 - tanh_val * tanh_val
    ) * gelu_scale * (1.0 + 3.0 * gelu_cubic * entries * entries)
    return (act_val, slope_val)


def layer_stats(summed):
    center = summed - jnp.mean(summed, axis=-1, keepdims=True)
    variance = jnp.mean(center * center, axis=-1, keepdims=True)
    inv_std = lax.rsqrt(variance + 1e-06)
    return (center * inv_std, inv_std)


def lower_mask(row_count):
    row_ids = lax.broadcasted_iota(jnp.int32, (row_count, row_count), 0)
    col_ids = lax.broadcasted_iota(jnp.int32, (row_count, row_count), 1)
    return (row_ids >= col_ids).astype(jnp.float32)


def inner_update(inner_state, key_mb, value_mb, rate_mb, norm_gain, norm_shift):
    weight_one, bias_one, weight_two, bias_two = inner_state
    hidden_pre = matmul_high(key_mb, weight_one) + bias_one
    hidden_act, hidden_slope = gelu_pair(hidden_pre)
    output_pre = matmul_high(hidden_act, weight_two) + bias_two
    normed, inv_std = layer_stats(output_pre)
    residual_err = norm_gain * normed + norm_shift - (value_mb - key_mb)
    scaled_err = residual_err * norm_gain
    grad_two = inv_std * (
        scaled_err
        - jnp.mean(scaled_err, axis=-1, keepdims=True)
        - normed * jnp.mean(scaled_err * normed, axis=-1, keepdims=True)
    )
    grad_one = matmul_high(grad_two, weight_two.T) * hidden_slope
    grad_one = grad_one * rate_mb[:, None]
    grad_two = grad_two * rate_mb[:, None]
    new_state = (
        weight_one - matmul_high(key_mb.T, grad_one),
        bias_one - jnp.sum(grad_one, axis=0),
        weight_two - matmul_high(hidden_act.T, grad_two),
        bias_two - jnp.sum(grad_two, axis=0),
    )
    return ((grad_one, hidden_act, grad_two), new_state)


def query_side(inner_state, query_mb, key_mb, grad_pack, norm_gain, norm_shift):
    weight_one, bias_one, weight_two, bias_two = inner_state
    grad_one, hidden_act, grad_two = grad_pack
    causal = lower_mask(query_mb.shape[0])
    first_kernel = (matmul_high(query_mb, key_mb.T) + 1.0) * causal
    query_pre = matmul_high(query_mb, weight_one) + bias_one - matmul_high(first_kernel, grad_one)
    query_act, unused_slope = gelu_pair(query_pre)
    second_kernel = (matmul_high(query_act, hidden_act.T) + 1.0) * causal
    query_out = matmul_high(query_act, weight_two) + bias_two - matmul_high(second_kernel, grad_two)
    normed, unused_inv = layer_stats(query_out)
    return query_mb + norm_gain * normed + norm_shift


def chain_scan(
    keep_queries, inner_state, queries, key_rows, values, rate_vals, norm_gain, norm_shift
):

    def stepper(loop_state, inputs):
        query_mb, key_mb, value_mb, rate_mb = inputs
        grad_pack, new_state = inner_update(
            loop_state, key_mb, value_mb, rate_mb, norm_gain, norm_shift
        )
        return (
            new_state,
            query_side(loop_state, query_mb, key_mb, grad_pack, norm_gain, norm_shift),
        )

    return lax.scan(stepper, inner_state, (queries, key_rows, values, rate_vals))


def pad_heads(array_in, total_heads, fill_value):
    extra = total_heads - array_in.shape[0]
    filler = jnp.full((extra,) + array_in.shape[1:], fill_value, array_in.dtype)
    return jnp.concatenate([array_in, filler], axis=0)


LANE = 128
MESH_ID = pl.DeviceIdType.MESH


def dot_nn(left, right):
    return lax.dot_general(
        left, right, (((1,), (0,)), ((), ())), preferred_element_type=jnp.float32
    )


def dot_nt(left, right):
    return lax.dot_general(
        left, right, (((1,), (1,)), ((), ())), preferred_element_type=jnp.float32
    )


def dot_tn(left, right):
    return lax.dot_general(
        left, right, (((0,), (0,)), ((), ())), preferred_element_type=jnp.float32
    )


def gelu_only(entries):
    inner_arg = gelu_scale * (entries + gelu_cubic * entries * entries * entries)
    return 0.5 * entries * (1.0 + jnp.tanh(inner_arg))


def half_mean(cells, left):
    first = jnp.sum(jnp.where(left, cells, 0.0), axis=-1, keepdims=True)
    second = jnp.sum(jnp.where(left, 0.0, cells), axis=-1, keepdims=True)
    return jnp.where(left, first, second) * (1.0 / HD)


def half_stats(summed, left):
    center = summed - half_mean(summed, left)
    inv_std = lax.rsqrt(half_mean(center * center, left) + 1e-06)
    return (center * inv_std, inv_std)


def split_heads(cells, left):
    wide = cells.astype(jnp.float32)
    return jnp.concatenate(
        [jnp.where(left, wide, 0.0), jnp.where(left, 0.0, wide)], axis=0
    ).astype(cells.dtype)


def fused_kernel(
    aqkv,
    iqkv,
    rate,
    first_w,
    second_w,
    out_w,
    seg,
    length,
    gate,
    gain,
    shift,
    first_b,
    second_b,
    out,
    a_rows,
    i_rows,
    rates,
    fw,
    sw,
    ow,
    w1m,
    w1b,
    w2m,
    w2b,
    b1,
    b2,
    gate_s,
    gain_s,
    shift_s,
    rate_a,
    rate_b,
    bias,
    inner,
    comb,
    gathered,
    parts,
    arrived,
    total,
    landed,
    load_sem,
    y_send,
    y_recv,
    back_send,
    back_recv,
    z_send,
    z_recv,
    own_sem,
    r_send,
    r_recv,
    t_send,
    t_recv,
):
    slabs, _, seq, _ = a_rows.shape
    tok = aqkv.shape[2]
    hidden = first_b.shape[1]
    count = lax.axis_size("head")
    c = lax.axis_index("ctx")
    h = lax.axis_index("head")
    v = lax.axis_index("video")
    other = 1 - c
    mine = pl.multiple_of(c * tok, tok)
    theirs = pl.multiple_of(other * tok, tok)
    pairs_heads = 2 * slabs

    def columns(owner, slab):
        return pl.ds(pl.multiple_of((owner * slabs + slab) * LANE, LANE), LANE)

    loads = []
    for slab in range(slabs):
        loads.append(
            pltpu.make_async_copy(
                iqkv.at[:, 0, :, columns(c, slab)],
                i_rows.at[slab, :, pl.ds(mine, tok), :],
                load_sem.at[slab],
            )
        )
    loads.append(pltpu.make_async_copy(rate, rates.at[c], load_sem.at[2 * slabs]))
    loads.append(
        pltpu.make_async_copy(
            first_w.at[pl.ds(c * pairs_heads, pairs_heads)], fw, load_sem.at[2 * slabs + 1]
        )
    )
    loads.append(
        pltpu.make_async_copy(
            second_w.at[pl.ds(c * pairs_heads, pairs_heads)], sw, load_sem.at[2 * slabs + 2]
        )
    )
    a_loads = [
        pltpu.make_async_copy(
            aqkv.at[:, 0, :, columns(c, slab)],
            a_rows.at[slab, :, pl.ds(mine, tok), :],
            load_sem.at[slabs + slab],
        )
        for slab in range(slabs)
    ]
    ow_load = pltpu.make_async_copy(out_w, ow, load_sem.at[2 * slabs + 3])
    for copy in loads + a_loads + [ow_load]:
        copy.start()

    barrier = pltpu.get_barrier_semaphore()
    pl.semaphore_signal(
        barrier, inc=1, device_id={"ctx": other}, device_id_type=MESH_ID
    )
    everyone = count * count
    place = h * count + v
    for step in range(1, everyone):
        peer = lax.rem(place + step, everyone)
        pl.semaphore_signal(
            barrier,
            inc=1,
            device_id={"head": peer // count, "video": lax.rem(peer, count)},
            device_id_type=MESH_ID,
        )
    pl.semaphore_wait(barrier, everyone)

    def to_partner(src, dst, send, recv):
        return pltpu.make_async_remote_copy(
            src_ref=src,
            dst_ref=dst,
            send_sem=send,
            recv_sem=recv,
            device_id={"ctx": other},
            device_id_type=MESH_ID,
        )

    rate_out = to_partner(
        rate, rates.at[c], y_send.at[2 * slabs], y_recv.at[2 * slabs]
    )
    rate_out.start()
    i_out = [
        to_partner(
            iqkv.at[:, 0, :, columns(other, slab)],
            i_rows.at[slab, :, pl.ds(mine, tok), :],
            y_send.at[slab],
            y_recv.at[slab],
        )
        for slab in range(slabs)
    ]
    a_out = [
        to_partner(
            aqkv.at[:, 0, :, columns(other, slab)],
            a_rows.at[slab, :, pl.ds(mine, tok), :],
            y_send.at[slabs + slab],
            y_recv.at[slabs + slab],
        )
        for slab in range(slabs)
    ]
    for first, second in zip(i_out, a_out):
        first.start()
        second.start()

    seq_ids = lax.broadcasted_iota(jnp.int32, (seq, seq), 1)
    row_ids = lax.broadcasted_iota(jnp.int32, (seq, seq), 0)
    len_val = length[0]
    segs = jnp.broadcast_to(seg[...].astype(jnp.float32), (seq, seq))
    allowed = (segs == segs.T) & ((seq_ids < len_val) | (seq_ids == row_ids))
    bias[...] = jnp.where(allowed, 0.0, -1e30)
    live = (lax.broadcasted_iota(jnp.int32, (seq, LANE), 0) < len_val).astype(jnp.float32)
    left = lax.broadcasted_iota(jnp.int32, (MB, LANE), 1) < HD
    left_seq = lax.broadcasted_iota(jnp.int32, (seq, LANE), 1) < HD
    tri = lax.broadcasted_iota(jnp.int32, (MB, MB), 0) >= lax.broadcasted_iota(
        jnp.int32, (MB, MB), 1
    )
    tri = tri.astype(jnp.float32)
    tri_pair = jnp.concatenate([tri, tri], axis=0)

    gate_s[...] = jnp.tanh(gate[...].reshape(1, gate.shape[0]))

    for copy in loads:
        copy.wait()

    def pair_row(ref, head):
        return jnp.concatenate([ref[pl.ds(head, 1), :], ref[pl.ds(head + 1, 1), :]], axis=1)

    for slab in range(slabs):
        head = c * pairs_heads + 2 * slab
        gain_s[slab] = pair_row(gain, head)
        shift_s[slab] = pair_row(shift, head)
        b1[slab] = pair_row(first_b, head)
        b2[slab] = pair_row(second_b, head)
        for raw, kept, used in ((fw, w1m, w1b), (sw, w2m, w2b)):
            upper, lower = raw[2 * slab], raw[2 * slab + 1]
            kept[slab, 0:HD] = upper.astype(jnp.float32)
            kept[slab, HD:LANE] = lower.astype(jnp.float32)
            used[slab] = jnp.zeros_like(used[slab])
            used[slab, 0:HD, 0:hidden] = upper
            used[slab, HD:LANE, hidden : 2 * hidden] = lower

    rate_out.wait_recv()
    for slab in range(slabs):
        head = c * pairs_heads + 2 * slab
        for part in range(seq // tok):
            rows = slice(part * tok, (part + 1) * tok)
            for ahead, store in ((0, rate_a), (1, rate_b)):
                row = rates[part, head + ahead]
                store[slab, rows] = jnp.broadcast_to(row, (LANE, tok)).T * live[rows]

    def inner_step(slab, row):
        rows = pl.ds(row, MB)
        query, key, value = (i_rows[slab, kind, rows, :] for kind in range(3))
        query_f = query.astype(jnp.float32)
        key_f = key.astype(jnp.float32)
        value_f = value.astype(jnp.float32)
        norm_gain = gain_s[slab]
        norm_shift = shift_s[slab]
        weight_one = w1b[slab]
        weight_two = w2b[slab]
        bias_one = b1[slab]
        bias_two = b2[slab]
        pre = dot_nn(jnp.concatenate([key, query], axis=0), weight_one) + bias_one
        hidden_act, slope = gelu_pair(pre[:MB])
        hidden_b = hidden_act.astype(jnp.bfloat16)
        normed, inv_std = half_stats(dot_nt(hidden_b, weight_two) + bias_two, left)
        scaled = (norm_gain * normed + norm_shift - (value_f - key_f)) * norm_gain
        grad_two = inv_std * (
            scaled - half_mean(scaled, left) - normed * half_mean(scaled * normed, left)
        )
        e_a = rate_a[slab, rows, :]
        e_b = rate_b[slab, rows, :]
        wide = [e_a] * (hidden // LANE) + [e_b] * (hidden // LANE)
        grad_one = dot_nn(grad_two.astype(jnp.bfloat16), weight_two) * slope
        grad_one = grad_one * jnp.concatenate(wide, axis=1)
        grad_two = grad_two * jnp.where(left, e_a, e_b)
        one_b = grad_one.astype(jnp.bfloat16)
        two_b = grad_two.astype(jnp.bfloat16)

        first_kernel = (dot_nt(split_heads(query, left), key) + 1.0) * tri_pair
        first_kernel = first_kernel.astype(jnp.bfloat16)
        fix = jnp.concatenate(
            [
                dot_nn(first_kernel[:MB], one_b[:, :hidden]),
                dot_nn(first_kernel[MB:], one_b[:, hidden:]),
            ],
            axis=1,
        )
        query_act = gelu_only(pre[MB:] - fix).astype(jnp.bfloat16)
        second_kernel = jnp.concatenate(
            [
                dot_nt(query_act[:, :hidden], hidden_b[:, :hidden]),
                dot_nt(query_act[:, hidden:], hidden_b[:, hidden:]),
            ],
            axis=0,
        )
        second_kernel = ((second_kernel + 1.0) * tri_pair).astype(jnp.bfloat16)
        fix_two = dot_nn(second_kernel, two_b)
        fix_two = jnp.where(left, fix_two[:MB], fix_two[MB:])
        query_out = dot_nt(query_act, weight_two) + bias_two - fix_two
        normed_out, _ = half_stats(query_out, left)
        inner[slab, rows, :] = query_f + norm_gain * normed_out + norm_shift

        for kept, used, change in (
            (w1m, w1b, dot_tn(key, one_b)),
            (w2m, w2b, dot_tn(two_b, hidden_b)),
        ):
            upper = kept[slab, 0:HD] - change[:HD, :hidden]
            lower = kept[slab, HD:LANE] - change[HD:, hidden:]
            kept[slab, 0:HD] = upper
            kept[slab, HD:LANE] = lower
            used[slab, 0:HD, 0:hidden] = upper.astype(jnp.bfloat16)
            used[slab, HD:LANE, hidden : 2 * hidden] = lower.astype(jnp.bfloat16)
        b1[slab] = bias_one - jnp.sum(grad_one, axis=0, keepdims=True)
        b2[slab] = bias_two - jnp.sum(grad_two, axis=0, keepdims=True)

    def to_video(src, video, spot, step):
        return pltpu.make_async_remote_copy(
            src_ref=src,
            dst_ref=gathered.at[v, spot],
            send_sem=z_send.at[spot, step - 1],
            recv_sem=z_recv.at[spot, step - 1],
            device_id={"video": video},
            device_id_type=MESH_ID,
        )

    def spread(src, spot):
        copies = []
        for step in range(1, count):
            copy = to_video(src, lax.rem(v + step, count), spot, step)
            copy.start()
            copies.append(copy)
        return copies

    z_out = []
    backs = []
    owns = []
    for slab in range(slabs):
        i_out[slab].wait_recv()

        def batch_step(batch, carry, slab=slab):
            inner_step(slab, pl.multiple_of(batch * MB, MB))
            return carry

        lax.fori_loop(0, seq // MB, batch_step, 0, unroll=True)
        a_loads[slab].wait()
        a_out[slab].wait_recv()
        query, key, value = (a_rows[slab, kind] for kind in range(3))
        scores = dot_nt(split_heads(query, left_seq), key) * HD ** (-0.5)
        halves = []
        for part in range(2):
            mine_scores = scores[part * seq : (part + 1) * seq] + bias[...]
            top = jnp.max(mine_scores, axis=-1, keepdims=True)
            weights = jnp.exp(mine_scores - top)
            mass = jnp.sum(weights, axis=-1, keepdims=True)
            halves.append(dot_nn(weights.astype(jnp.bfloat16), value) / mass)
        attended = jnp.where(left_seq, halves[0], halves[1])
        gate_row = gate_s[:, columns(c, slab)]
        comb[slab] = ((attended + gate_row * inner[slab]) * live).astype(jnp.bfloat16)
        spot = c * slabs + slab
        back = to_partner(
            comb.at[slab, pl.ds(theirs, tok), :],
            gathered.at[v, spot],
            back_send.at[slab],
            back_recv.at[slab],
        )
        back.start()
        backs.append(back)
        own = pltpu.make_async_copy(
            comb.at[slab, pl.ds(mine, tok), :], gathered.at[v, spot], own_sem.at[slab]
        )
        own.start()
        owns.append(own)
        z_out += spread(comb.at[slab, pl.ds(mine, tok), :], spot)
        if slab:
            backs[slab - 1].wait_recv()
            far = other * slabs + slab - 1
            z_out += spread(gathered.at[v, far], far)
    backs[slabs - 1].wait_recv()
    far = other * slabs + slabs - 1
    z_out += spread(gathered.at[v, far], far)
    for own in owns:
        own.wait()
    ow_load.wait()

    def owner_of(video):
        return lax.rem(video, 2) * (count // 2) + video // 2

    def video_of(head):
        return lax.rem(head, count // 2) * 2 + head // (count // 2)

    for step in range(1, count):
        source = lax.rem(v + count - step, count)
        for spot in range(2 * slabs):
            pltpu.make_async_remote_copy(
                src_ref=gathered.at[source, spot],
                dst_ref=gathered.at[source, spot],
                send_sem=z_send.at[spot, step - 1],
                recv_sem=z_recv.at[spot, step - 1],
                device_id={"video": source},
                device_id_type=MESH_ID,
            ).wait_recv()
    rows_all = jnp.concatenate(
        [
            jnp.concatenate([gathered[video, spot] for spot in range(2 * slabs)], axis=1)
            for video in range(count)
        ],
        axis=0,
    )
    chunks, _, _, chunk = parts.shape
    r_out = []
    for at in range(chunks):
        piece = dot_nn(rows_all, ow[:, at * chunk : (at + 1) * chunk]).astype(jnp.bfloat16)
        for video in range(count):
            parts[at, video] = piece[video * tok : (video + 1) * tok]
        for step in range(count - 1, 0, -1):
            head = lax.rem(h + step, count)
            copy = pltpu.make_async_remote_copy(
                src_ref=parts.at[at, video_of(head)],
                dst_ref=arrived.at[at, step - 1],
                send_sem=r_send.at[at, step - 1],
                recv_sem=r_recv.at[at, step - 1],
                device_id={"head": head},
                device_id_type=MESH_ID,
            )
            copy.start()
            r_out.append(copy)

    to_head, to_v = v, video_of(h)
    stays = (to_head == h) & (to_v == v)
    finals = []
    for at in range(chunks):
        for copy in r_out[at * (count - 1) : (at + 1) * (count - 1)]:
            copy.wait_recv()
        summed = parts[at, video_of(h)].astype(jnp.float32)
        for step in range(count - 1):
            summed = summed + arrived[at, step].astype(jnp.float32)
        total[at] = summed.astype(jnp.bfloat16)
        final = pltpu.make_async_remote_copy(
            src_ref=total.at[at],
            dst_ref=landed.at[at],
            send_sem=t_send.at[at],
            recv_sem=t_recv.at[at],
            device_id={"head": to_head, "video": to_v},
            device_id_type=MESH_ID,
        )

        @pl.when(stays)
        def _(at=at):
            landed[at] = total[at]

        @pl.when(jnp.logical_not(stays))
        def _(final=final):
            final.start()

        finals.append(final)

    @pl.when(jnp.logical_not(stays))
    def _():
        for final in finals:
            final.wait()

    for at in range(chunks):
        out[0, :, at * chunk : (at + 1) * chunk] = landed[at]

    for copy in [rate_out] + i_out + a_out + backs + z_out + r_out:
        copy.wait_send()


def fused_on_device(
    attention_qkv,
    inner_qkv,
    learn_rate,
    segment_id,
    video_length,
    gate_alpha,
    inner_gain,
    inner_shift,
    first_weight,
    first_bias,
    second_weight,
    second_bias,
    out_weight,
):
    tok = attention_qkv.shape[2]
    width_dev = attention_qkv.shape[3]
    count = lax.axis_size("head")
    ctx_count = lax.axis_size("ctx")
    seq = tok * ctx_count
    slabs = width_dev // LANE // ctx_count
    heads = width_dev // HD
    hidden = first_weight.shape[2]
    columns = out_weight.shape[1]
    chunk = 2 * LANE if columns % (2 * LANE) == 0 else columns
    chunks = columns // chunk
    half = jnp.bfloat16
    full = jnp.float32
    hbm = pl.BlockSpec(memory_space=pl.ANY)
    vmem = pl.BlockSpec(memory_space=pltpu.VMEM)
    smem = pl.BlockSpec(memory_space=pltpu.SMEM)
    dma = pltpu.SemaphoreType.DMA
    return pl.pallas_call(
        fused_kernel,
        out_shape=jax.ShapeDtypeStruct((1, tok, columns), half),
        in_specs=[hbm] * 6 + [vmem, smem] + [vmem] * 5,
        out_specs=vmem,
        scratch_shapes=[
            pltpu.VMEM((slabs, 3, seq, LANE), half),
            pltpu.VMEM((slabs, 3, seq, LANE), half),
            pltpu.VMEM((ctx_count, heads, 1, tok), full),
            pltpu.VMEM((2 * slabs,) + first_weight.shape[1:], half),
            pltpu.VMEM((2 * slabs,) + second_weight.shape[:0:-1], half),
            pltpu.VMEM(out_weight.shape, half),
            pltpu.VMEM((slabs, LANE, hidden), full),
            pltpu.VMEM((slabs, LANE, 2 * hidden), half),
            pltpu.VMEM((slabs, LANE, hidden), full),
            pltpu.VMEM((slabs, LANE, 2 * hidden), half),
            pltpu.VMEM((slabs, 1, 2 * hidden), full),
            pltpu.VMEM((slabs, 1, LANE), full),
            pltpu.VMEM((1, width_dev), full),
            pltpu.VMEM((slabs, 1, LANE), full),
            pltpu.VMEM((slabs, 1, LANE), full),
            pltpu.VMEM((slabs, seq, LANE), full),
            pltpu.VMEM((slabs, seq, LANE), full),
            pltpu.VMEM((seq, seq), full),
            pltpu.VMEM((slabs, seq, LANE), full),
            pltpu.VMEM((slabs, seq, LANE), half),
            pltpu.VMEM((count, 2 * slabs, tok, LANE), half),
            pltpu.VMEM((chunks, count, tok, chunk), half),
            pltpu.VMEM((chunks, count - 1, tok, chunk), half),
            pltpu.VMEM((chunks, tok, chunk), half),
            pltpu.VMEM((chunks, tok, chunk), half),
            dma((2 * slabs + 4,)),
            dma((2 * slabs + 1,)),
            dma((2 * slabs + 1,)),
            dma((slabs,)),
            dma((slabs,)),
            dma((2 * slabs, count - 1)),
            dma((2 * slabs, count - 1)),
            dma((slabs,)),
            dma((chunks, count - 1)),
            dma((chunks, count - 1)),
            dma((chunks,)),
            dma((chunks,)),
        ],
        compiler_params=pltpu.CompilerParams(
            collective_id=0, has_side_effects=True, vmem_limit_bytes=60 * 1024 * 1024
        ),
    )(
        attention_qkv,
        inner_qkv,
        learn_rate.transpose(1, 0, 2),
        first_weight,
        second_weight.transpose(0, 2, 1),
        out_weight,
        segment_id,
        video_length,
        gate_alpha,
        inner_gain,
        inner_shift,
        first_bias,
        second_bias,
    )


def general_on_device(
    attention_qkv,
    inner_qkv,
    learn_rate,
    segment_id,
    video_length,
    gate_alpha,
    inner_gain,
    inner_shift,
    first_weight,
    first_bias,
    second_weight,
    second_bias,
    out_weight,
):
    tok_count = attention_qkv.shape[2]
    width_dev = attention_qkv.shape[3]
    heads_dev = width_dev // HD
    ctx_index = lax.axis_index("ctx")
    ctx_count = lax.axis_size("ctx")
    positions = ctx_index * tok_count + jnp.arange(tok_count, dtype=jnp.int32)
    length_val = video_length[0]
    live_rows = (positions < length_val).astype(jnp.float32)
    kv_pair = attention_qkv[1:, 0]
    kv_wide = with_halo(kv_pair, (("ctx", 1),), tok_count)
    key_pos = (ctx_index - 1) * tok_count + jnp.arange(3 * tok_count, dtype=jnp.int32)
    seg_row = segment_id[0]
    fill_ids = jnp.full((tok_count,), -1, jnp.int32)
    seg_pad = jnp.concatenate([fill_ids, seg_row, fill_ids])
    key_seg = lax.dynamic_slice_in_dim(seg_pad, ctx_index * tok_count, 3 * tok_count, 0)
    query_seg = lax.dynamic_slice_in_dim(seg_row, ctx_index * tok_count, tok_count, 0)
    allowed = (key_seg[None, :] == query_seg[:, None]) & (
        (key_pos[None, :] < length_val) | (key_pos[None, :] == positions[:, None])
    )
    query_heads = attention_qkv[0, 0].reshape(tok_count, heads_dev, HD)
    key_heads = kv_wide[0].reshape(3 * tok_count, heads_dev, HD)
    value_heads = kv_wide[1].reshape(3 * tok_count, heads_dev, HD)
    scores = jnp.einsum(
        "qhd,khd->hqk", query_heads, key_heads, preferred_element_type=jnp.float32
    ) * HD ** (-0.5)
    scores = jnp.where(allowed[None], scores, -1e30)
    row_max = jnp.max(scores, axis=-1, keepdims=True)
    exp_scores = jnp.exp(scores - row_max)
    soft_weights = (exp_scores / jnp.sum(exp_scores, axis=-1, keepdims=True)).astype(jnp.bfloat16)
    attended = jnp.einsum(
        "hqk,khd->qhd", soft_weights, value_heads, preferred_element_type=jnp.float32
    ).reshape(tok_count, width_dev)
    init_state = (
        first_weight.astype(jnp.float32),
        first_bias,
        second_weight.astype(jnp.float32),
        second_bias,
    )
    rate_rows = learn_rate[0] * live_rows[None, :]
    heads_each = -(-heads_dev // ctx_count)
    heads_padded = heads_each * ctx_count
    rows_heads = inner_qkv[:, 0].reshape(3, tok_count, heads_dev, HD)
    rows_padded = jnp.concatenate(
        [rows_heads, jnp.zeros((3, tok_count, heads_padded - heads_dev, HD), rows_heads.dtype)],
        axis=2,
    )
    rates_padded = pad_heads(rate_rows, heads_padded, 0.0)
    whole_rows = lax.all_to_all(rows_padded, "ctx", split_axis=2, concat_axis=1, tiled=True)
    whole_rates = lax.all_to_all(rates_padded, "ctx", split_axis=0, concat_axis=1, tiled=True)
    seq_count = whole_rows.shape[1]
    full_batches = seq_count // MB
    local_qkv = (
        whole_rows.astype(jnp.float32)
        .transpose(0, 2, 1, 3)
        .reshape(3, heads_each, full_batches, MB, HD)
    )
    local_rates = whole_rates.reshape(heads_each, full_batches, MB)
    first_head = ctx_index * heads_each
    local_gain = lax.dynamic_slice_in_dim(
        pad_heads(inner_gain, heads_padded, 1.0), first_head, heads_each, 0
    )
    local_shift = lax.dynamic_slice_in_dim(
        pad_heads(inner_shift, heads_padded, 0.0), first_head, heads_each, 0
    )
    local_state = tuple(
        (
            lax.dynamic_slice_in_dim(
                pad_heads(piece_arr, heads_padded, 0.0), first_head, heads_each, 0
            )
            for piece_arr in init_state
        )
    )
    unused_final, saved_local = jax.vmap(partial(chain_scan, True))(
        local_state, local_qkv[0], local_qkv[1], local_qkv[2], local_rates, local_gain, local_shift
    )
    out_rows = saved_local.reshape(heads_each, seq_count, HD).transpose(1, 0, 2)
    back_rows = lax.all_to_all(
        out_rows.astype(jnp.bfloat16), "ctx", split_axis=0, concat_axis=1, tiled=True
    ).astype(out_rows.dtype)
    inner_flat = back_rows[:, :heads_dev].reshape(tok_count, width_dev)
    combined = ((attended + jnp.tanh(gate_alpha) * inner_flat) * live_rows[:, None]).astype(
        jnp.bfloat16
    )
    terms = jnp.dot(
        combined,
        lax.all_gather(out_weight, "video", axis=1, tiled=True),
        preferred_element_type=jnp.float32,
    )
    mixed = lax.psum_scatter(terms.astype(jnp.bfloat16), "head", scatter_dimension=1, tiled=True)
    return mixed[None]


def solution(mesh):
    placed = (
        P(None, "video", "ctx", "head"),
        P(None, "video", "ctx", "head"),
        P("video", "head", "ctx"),
        P("video", None),
        P("video"),
        P("head"),
        P("head", None),
        P("head", None),
        P("head", None, None),
        P("head", None),
        P("head", None, None),
        P("head", None),
        P("head", "video"),
    )
    shape = mesh.shape
    fused = shape["ctx"] == 2 and shape["head"] == shape["video"] and shape["head"] % 2 == 0

    def on_device(*args):
        heads_dev = args[0].shape[3] // HD
        if fused and heads_dev % (2 * shape["ctx"]) == 0 and args[0].shape[2] % 128 == 0:
            return fused_on_device(*args)
        return general_on_device(*args)

    return jax.shard_map(
        on_device, mesh=mesh, in_specs=placed, out_specs=P("video", "ctx", "head"), check_vma=False
    )
```

```python
from functools import partial

import jax
import jax.numpy as jnp
from jax import lax
from jax.experimental import pallas as pl
from jax.experimental.pallas import tpu as pltpu
from jax.sharding import PartitionSpec as P

HD = 64
MB = 64


gelu_scale = 0.7978845608028654
gelu_cubic = 0.044715


def with_halo(cells, sides, width):
    for axis, dim in sides:
        count = lax.axis_size(axis)
        ends = count - 1
        head = lax.slice_in_dim(cells, 0, width, axis=dim)
        tail = lax.slice_in_dim(cells, cells.shape[dim] - width, cells.shape[dim], axis=dim)
        cells = jnp.concatenate(
            [
                lax.ppermute(tail, axis, [(i, (i + 1) % count) for i in range(ends)]),
                cells,
                lax.ppermute(head, axis, [((i + 1) % count, i) for i in range(ends)]),
            ],
            axis=dim,
        )
    return cells


def matmul_high(first_op, second_op):
    return jnp.matmul(first_op, second_op, precision=lax.Precision.HIGHEST)


def gelu_pair(entries):
    inner_arg = gelu_scale * (entries + gelu_cubic * entries * entries * entries)
    tanh_val = jnp.tanh(inner_arg)
    act_val = 0.5 * entries * (1.0 + tanh_val)
    slope_val = 0.5 * (1.0 + tanh_val) + 0.5 * entries * (
        1.0 - tanh_val * tanh_val
    ) * gelu_scale * (1.0 + 3.0 * gelu_cubic * entries * entries)
    return (act_val, slope_val)


def layer_stats(summed):
    center = summed - jnp.mean(summed, axis=-1, keepdims=True)
    variance = jnp.mean(center * center, axis=-1, keepdims=True)
    inv_std = lax.rsqrt(variance + 1e-06)
    return (center * inv_std, inv_std)


def lower_mask(row_count):
    row_ids = lax.broadcasted_iota(jnp.int32, (row_count, row_count), 0)
    col_ids = lax.broadcasted_iota(jnp.int32, (row_count, row_count), 1)
    return (row_ids >= col_ids).astype(jnp.float32)


def inner_update(inner_state, key_mb, value_mb, rate_mb, norm_gain, norm_shift):
    weight_one, bias_one, weight_two, bias_two = inner_state
    hidden_pre = matmul_high(key_mb, weight_one) + bias_one
    hidden_act, hidden_slope = gelu_pair(hidden_pre)
    output_pre = matmul_high(hidden_act, weight_two) + bias_two
    normed, inv_std = layer_stats(output_pre)
    residual_err = norm_gain * normed + norm_shift - (value_mb - key_mb)
    scaled_err = residual_err * norm_gain
    grad_two = inv_std * (
        scaled_err
        - jnp.mean(scaled_err, axis=-1, keepdims=True)
        - normed * jnp.mean(scaled_err * normed, axis=-1, keepdims=True)
    )
    grad_one = matmul_high(grad_two, weight_two.T) * hidden_slope
    grad_one = grad_one * rate_mb[:, None]
    grad_two = grad_two * rate_mb[:, None]
    new_state = (
        weight_one - matmul_high(key_mb.T, grad_one),
        bias_one - jnp.sum(grad_one, axis=0),
        weight_two - matmul_high(hidden_act.T, grad_two),
        bias_two - jnp.sum(grad_two, axis=0),
    )
    return ((grad_one, hidden_act, grad_two), new_state)


def query_side(inner_state, query_mb, key_mb, grad_pack, norm_gain, norm_shift):
    weight_one, bias_one, weight_two, bias_two = inner_state
    grad_one, hidden_act, grad_two = grad_pack
    causal = lower_mask(query_mb.shape[0])
    first_kernel = (matmul_high(query_mb, key_mb.T) + 1.0) * causal
    query_pre = matmul_high(query_mb, weight_one) + bias_one - matmul_high(first_kernel, grad_one)
    query_act, unused_slope = gelu_pair(query_pre)
    second_kernel = (matmul_high(query_act, hidden_act.T) + 1.0) * causal
    query_out = matmul_high(query_act, weight_two) + bias_two - matmul_high(second_kernel, grad_two)
    normed, unused_inv = layer_stats(query_out)
    return query_mb + norm_gain * normed + norm_shift


def chain_scan(
    keep_queries, inner_state, queries, key_rows, values, rate_vals, norm_gain, norm_shift
):

    def stepper(loop_state, inputs):
        query_mb, key_mb, value_mb, rate_mb = inputs
        grad_pack, new_state = inner_update(
            loop_state, key_mb, value_mb, rate_mb, norm_gain, norm_shift
        )
        return (
            new_state,
            query_side(loop_state, query_mb, key_mb, grad_pack, norm_gain, norm_shift),
        )

    return lax.scan(stepper, inner_state, (queries, key_rows, values, rate_vals))


def pad_heads(array_in, total_heads, fill_value):
    extra = total_heads - array_in.shape[0]
    filler = jnp.full((extra,) + array_in.shape[1:], fill_value, array_in.dtype)
    return jnp.concatenate([array_in, filler], axis=0)


LANE = 128
MESH_ID = pl.DeviceIdType.MESH


def dot_nn(left, right):
    return lax.dot_general(
        left, right, (((1,), (0,)), ((), ())), preferred_element_type=jnp.float32
    )


def dot_nt(left, right):
    return lax.dot_general(
        left, right, (((1,), (1,)), ((), ())), preferred_element_type=jnp.float32
    )


def dot_tn(left, right):
    return lax.dot_general(
        left, right, (((0,), (0,)), ((), ())), preferred_element_type=jnp.float32
    )


def gelu_only(entries):
    inner_arg = gelu_scale * (entries + gelu_cubic * entries * entries * entries)
    return 0.5 * entries * (1.0 + jnp.tanh(inner_arg))


def half_mean(cells, left):
    first = jnp.sum(jnp.where(left, cells, 0.0), axis=-1, keepdims=True)
    second = jnp.sum(jnp.where(left, 0.0, cells), axis=-1, keepdims=True)
    return jnp.where(left, first, second) * (1.0 / HD)


def half_stats(summed, left):
    center = summed - half_mean(summed, left)
    inv_std = lax.rsqrt(half_mean(center * center, left) + 1e-06)
    return (center * inv_std, inv_std)


def split_heads(cells, left):
    wide = cells.astype(jnp.float32)
    return jnp.concatenate(
        [jnp.where(left, wide, 0.0), jnp.where(left, 0.0, wide)], axis=0
    ).astype(cells.dtype)


def fused_kernel(
    aqkv,
    iqkv,
    rate,
    first_w,
    second_w,
    out_w,
    seg,
    length,
    gate,
    gain,
    shift,
    first_b,
    second_b,
    out,
    a_rows,
    i_rows,
    rates,
    fw,
    sw,
    ow,
    w1m,
    w1b,
    w2m,
    w2b,
    b1,
    b2,
    gate_s,
    gain_s,
    shift_s,
    rate_a,
    rate_b,
    bias,
    inner,
    comb,
    gathered,
    parts,
    arrived,
    total,
    landed,
    load_sem,
    y_send,
    y_recv,
    back_send,
    back_recv,
    z_send,
    z_recv,
    own_sem,
    r_send,
    r_recv,
    t_send,
    t_recv,
    low_sem,
    high_sem,
):
    slabs, _, seq, _ = a_rows.shape
    tok = aqkv.shape[2]
    hidden = first_b.shape[1]
    count = lax.axis_size("head")
    c = lax.axis_index("ctx")
    h = lax.axis_index("head")
    v = lax.axis_index("video")
    other = 1 - c
    mine = pl.multiple_of(c * tok, tok)
    theirs = pl.multiple_of(other * tok, tok)
    pairs_heads = 2 * slabs

    def columns(owner, slab):
        return pl.ds(pl.multiple_of((owner * slabs + slab) * LANE, LANE), LANE)

    loads = []
    for slab in range(slabs):
        loads.append(
            pltpu.make_async_copy(
                iqkv.at[:, 0, :, columns(c, slab)],
                i_rows.at[slab, :, pl.ds(mine, tok), :],
                load_sem.at[slab],
            )
        )
    loads.append(pltpu.make_async_copy(rate, rates.at[c], load_sem.at[2 * slabs]))
    loads.append(
        pltpu.make_async_copy(
            first_w.at[pl.ds(c * pairs_heads, pairs_heads)], fw, load_sem.at[2 * slabs + 1]
        )
    )
    loads.append(
        pltpu.make_async_copy(
            second_w.at[pl.ds(c * pairs_heads, pairs_heads)], sw, load_sem.at[2 * slabs + 2]
        )
    )
    a_loads = [
        pltpu.make_async_copy(
            aqkv.at[:, 0, :, columns(c, slab)],
            a_rows.at[slab, :, pl.ds(mine, tok), :],
            load_sem.at[slabs + slab],
        )
        for slab in range(slabs)
    ]
    ow_load = pltpu.make_async_copy(out_w, ow, load_sem.at[2 * slabs + 3])
    for copy in loads + a_loads + [ow_load]:
        copy.start()

    barrier = pltpu.get_barrier_semaphore()
    pl.semaphore_signal(
        barrier, inc=1, device_id={"ctx": other}, device_id_type=MESH_ID
    )
    below, above = v > 0, v < count - 1
    for step in range(1, count):
        pl.semaphore_signal(
            barrier,
            inc=1,
            device_id={"head": lax.rem(h + step, count)},
            device_id_type=MESH_ID,
        )

    def tell(semaphore, inside, video):
        @pl.when(inside)
        def _():
            pl.semaphore_signal(
                semaphore, inc=1, device_id={"video": video}, device_id_type=MESH_ID
            )

    tell(barrier, below, v - 1)
    tell(barrier, above, v + 1)
    pl.semaphore_wait(barrier, count + (v + count - 1) // count + (2 * count - 2 - v) // count)

    def to_partner(src, dst, send, recv):
        return pltpu.make_async_remote_copy(
            src_ref=src,
            dst_ref=dst,
            send_sem=send,
            recv_sem=recv,
            device_id={"ctx": other},
            device_id_type=MESH_ID,
        )

    rate_out = to_partner(
        rate, rates.at[c], y_send.at[2 * slabs], y_recv.at[2 * slabs]
    )
    rate_out.start()
    i_out = [
        to_partner(
            iqkv.at[:, 0, :, columns(other, slab)],
            i_rows.at[slab, :, pl.ds(mine, tok), :],
            y_send.at[slab],
            y_recv.at[slab],
        )
        for slab in range(slabs)
    ]
    a_out = [
        to_partner(
            aqkv.at[:, 0, :, columns(other, slab)],
            a_rows.at[slab, :, pl.ds(mine, tok), :],
            y_send.at[slabs + slab],
            y_recv.at[slabs + slab],
        )
        for slab in range(slabs)
    ]
    for first, second in zip(i_out, a_out):
        first.start()
        second.start()

    for semaphore, first, video, last in (
        (low_sem, below, v + 1, above),
        (high_sem, above, v - 1, below),
    ):

        @pl.when(first)
        def _(semaphore=semaphore):
            pl.semaphore_wait(semaphore, 1)

        tell(semaphore, last, video)

    seq_ids = lax.broadcasted_iota(jnp.int32, (seq, seq), 1)
    row_ids = lax.broadcasted_iota(jnp.int32, (seq, seq), 0)
    len_val = length[0]
    segs = jnp.broadcast_to(seg[...].astype(jnp.float32), (seq, seq))
    allowed = (segs == segs.T) & ((seq_ids < len_val) | (seq_ids == row_ids))
    bias[...] = jnp.where(allowed, 0.0, -1e30)
    live = (lax.broadcasted_iota(jnp.int32, (seq, LANE), 0) < len_val).astype(jnp.float32)
    left = lax.broadcasted_iota(jnp.int32, (MB, LANE), 1) < HD
    left_seq = lax.broadcasted_iota(jnp.int32, (seq, LANE), 1) < HD
    tri = lax.broadcasted_iota(jnp.int32, (MB, MB), 0) >= lax.broadcasted_iota(
        jnp.int32, (MB, MB), 1
    )
    tri = tri.astype(jnp.float32)
    tri_pair = jnp.concatenate([tri, tri], axis=0)

    gate_s[...] = jnp.tanh(gate[...].reshape(1, gate.shape[0]))

    for copy in loads:
        copy.wait()

    def pair_row(ref, head):
        return jnp.concatenate([ref[pl.ds(head, 1), :], ref[pl.ds(head + 1, 1), :]], axis=1)

    for slab in range(slabs):
        head = c * pairs_heads + 2 * slab
        gain_s[slab] = pair_row(gain, head)
        shift_s[slab] = pair_row(shift, head)
        b1[slab] = pair_row(first_b, head)
        b2[slab] = pair_row(second_b, head)
        for raw, kept, used in ((fw, w1m, w1b), (sw, w2m, w2b)):
            upper, lower = raw[2 * slab], raw[2 * slab + 1]
            kept[slab, 0:HD] = upper.astype(jnp.float32)
            kept[slab, HD:LANE] = lower.astype(jnp.float32)
            used[slab] = jnp.zeros_like(used[slab])
            used[slab, 0:HD, 0:hidden] = upper
            used[slab, HD:LANE, hidden : 2 * hidden] = lower

    rate_out.wait_recv()
    for slab in range(slabs):
        head = c * pairs_heads + 2 * slab
        for part in range(seq // tok):
            rows = slice(part * tok, (part + 1) * tok)
            for ahead, store in ((0, rate_a), (1, rate_b)):
                row = rates[part, head + ahead]
                store[slab, rows] = jnp.broadcast_to(row, (LANE, tok)).T * live[rows]

    def inner_step(slab, row):
        rows = pl.ds(row, MB)
        query, key, value = (i_rows[slab, kind, rows, :] for kind in range(3))
        query_f = query.astype(jnp.float32)
        key_f = key.astype(jnp.float32)
        value_f = value.astype(jnp.float32)
        norm_gain = gain_s[slab]
        norm_shift = shift_s[slab]
        weight_one = w1b[slab]
        weight_two = w2b[slab]
        bias_one = b1[slab]
        bias_two = b2[slab]
        pre = dot_nn(jnp.concatenate([key, query], axis=0), weight_one) + bias_one
        hidden_act, slope = gelu_pair(pre[:MB])
        hidden_b = hidden_act.astype(jnp.bfloat16)
        normed, inv_std = half_stats(dot_nt(hidden_b, weight_two) + bias_two, left)
        scaled = (norm_gain * normed + norm_shift - (value_f - key_f)) * norm_gain
        grad_two = inv_std * (
            scaled - half_mean(scaled, left) - normed * half_mean(scaled * normed, left)
        )
        e_a = rate_a[slab, rows, :]
        e_b = rate_b[slab, rows, :]
        wide = [e_a] * (hidden // LANE) + [e_b] * (hidden // LANE)
        grad_one = dot_nn(grad_two.astype(jnp.bfloat16), weight_two) * slope
        grad_one = grad_one * jnp.concatenate(wide, axis=1)
        grad_two = grad_two * jnp.where(left, e_a, e_b)
        one_b = grad_one.astype(jnp.bfloat16)
        two_b = grad_two.astype(jnp.bfloat16)

        first_kernel = (dot_nt(split_heads(query, left), key) + 1.0) * tri_pair
        first_kernel = first_kernel.astype(jnp.bfloat16)
        fix = jnp.concatenate(
            [
                dot_nn(first_kernel[:MB], one_b[:, :hidden]),
                dot_nn(first_kernel[MB:], one_b[:, hidden:]),
            ],
            axis=1,
        )
        query_act = gelu_only(pre[MB:] - fix).astype(jnp.bfloat16)
        second_kernel = jnp.concatenate(
            [
                dot_nt(query_act[:, :hidden], hidden_b[:, :hidden]),
                dot_nt(query_act[:, hidden:], hidden_b[:, hidden:]),
            ],
            axis=0,
        )
        second_kernel = ((second_kernel + 1.0) * tri_pair).astype(jnp.bfloat16)
        fix_two = dot_nn(second_kernel, two_b)
        fix_two = jnp.where(left, fix_two[:MB], fix_two[MB:])
        query_out = dot_nt(query_act, weight_two) + bias_two - fix_two
        normed_out, _ = half_stats(query_out, left)
        inner[slab, rows, :] = query_f + norm_gain * normed_out + norm_shift

        for kept, used, change in (
            (w1m, w1b, dot_tn(key, one_b)),
            (w2m, w2b, dot_tn(two_b, hidden_b)),
        ):
            upper = kept[slab, 0:HD] - change[:HD, :hidden]
            lower = kept[slab, HD:LANE] - change[HD:, hidden:]
            kept[slab, 0:HD] = upper
            kept[slab, HD:LANE] = lower
            used[slab, 0:HD, 0:hidden] = upper.astype(jnp.bfloat16)
            used[slab, HD:LANE, hidden : 2 * hidden] = lower.astype(jnp.bfloat16)
        b1[slab] = bias_one - jnp.sum(grad_one, axis=0, keepdims=True)
        b2[slab] = bias_two - jnp.sum(grad_two, axis=0, keepdims=True)

    def to_video(src, video, spot, step):
        return pltpu.make_async_remote_copy(
            src_ref=src,
            dst_ref=gathered.at[v, spot],
            send_sem=z_send.at[spot, step - 1],
            recv_sem=z_recv.at[spot, step - 1],
            device_id={"video": video},
            device_id_type=MESH_ID,
        )

    def spread(src, spot):
        copies = []
        for step in range(1, count):
            copy = to_video(src, lax.rem(v + step, count), spot, step)
            copy.start()
            copies.append(copy)
        return copies

    z_out = []
    backs = []
    owns = []
    for slab in range(slabs):
        i_out[slab].wait_recv()

        def batch_step(batch, carry, slab=slab):
            inner_step(slab, pl.multiple_of(batch * MB, MB))
            return carry

        lax.fori_loop(0, seq // MB, batch_step, 0, unroll=True)
        a_loads[slab].wait()
        a_out[slab].wait_recv()
        query, key, value = (a_rows[slab, kind] for kind in range(3))
        scores = dot_nt(split_heads(query, left_seq), key) * HD ** (-0.5)
        halves = []
        for part in range(2):
            mine_scores = scores[part * seq : (part + 1) * seq] + bias[...]
            top = jnp.max(mine_scores, axis=-1, keepdims=True)
            weights = jnp.exp(mine_scores - top)
            mass = jnp.sum(weights, axis=-1, keepdims=True)
            halves.append(dot_nn(weights.astype(jnp.bfloat16), value) / mass)
        attended = jnp.where(left_seq, halves[0], halves[1])
        gate_row = gate_s[:, columns(c, slab)]
        comb[slab] = ((attended + gate_row * inner[slab]) * live).astype(jnp.bfloat16)
        spot = c * slabs + slab
        back = to_partner(
            comb.at[slab, pl.ds(theirs, tok), :],
            gathered.at[v, spot],
            back_send.at[slab],
            back_recv.at[slab],
        )
        back.start()
        backs.append(back)
        own = pltpu.make_async_copy(
            comb.at[slab, pl.ds(mine, tok), :], gathered.at[v, spot], own_sem.at[slab]
        )
        own.start()
        owns.append(own)
        z_out += spread(comb.at[slab, pl.ds(mine, tok), :], spot)
        if slab:
            backs[slab - 1].wait_recv()
            far = other * slabs + slab - 1
            z_out += spread(gathered.at[v, far], far)
    backs[slabs - 1].wait_recv()
    far = other * slabs + slabs - 1
    z_out += spread(gathered.at[v, far], far)
    for own in owns:
        own.wait()
    ow_load.wait()

    def owner_of(video):
        return lax.rem(video, 2) * (count // 2) + video // 2

    def video_of(head):
        return lax.rem(head, count // 2) * 2 + head // (count // 2)

    chunks, _, _, chunk = parts.shape
    toward = 1 - 2 * (v // (count // 2))

    def part_copy(video, at):
        head = owner_of(video)
        ahead = lax.rem(head - h + count, count)
        slot = lax.rem(ahead + count - 1, count)
        return head, pltpu.make_async_remote_copy(
            src_ref=parts.at[at, video],
            dst_ref=arrived.at[at, slot],
            send_sem=r_send.at[at, slot],
            recv_sem=r_recv.at[at, slot],
            device_id={"head": head},
            device_id_type=MESH_ID,
        )

    videos = []
    for near in range(count):
        video = lax.rem(v + toward * near + count, count)
        videos.append(video)
        if near:
            step = lax.rem(v - video + count, count)
            for spot in range(2 * slabs):
                pltpu.make_async_remote_copy(
                    src_ref=gathered.at[video, spot],
                    dst_ref=gathered.at[video, spot],
                    send_sem=z_send.at[spot, step - 1],
                    recv_sem=z_recv.at[spot, step - 1],
                    device_id={"video": video},
                    device_id_type=MESH_ID,
                ).wait_recv()
        rows_video = jnp.concatenate(
            [gathered[video, spot] for spot in range(2 * slabs)], axis=1
        )
        for at in range(chunks):
            piece = dot_nn(rows_video, ow[:, at * chunk : (at + 1) * chunk])
            parts[at, video] = piece.astype(jnp.bfloat16)
            head, copy = part_copy(video, at)

            @pl.when(head != h)
            def _(copy=copy):
                copy.start()

    to_head, to_v = v, video_of(h)
    stays = (to_head == h) & (to_v == v)
    finals = []
    for at in range(chunks):
        for step in range(1, count):
            pltpu.make_async_remote_copy(
                src_ref=arrived.at[at, step - 1],
                dst_ref=arrived.at[at, step - 1],
                send_sem=r_send.at[at, step - 1],
                recv_sem=r_recv.at[at, step - 1],
                device_id={"head": lax.rem(h + step, count)},
                device_id_type=MESH_ID,
            ).wait_recv()
        summed = parts[at, video_of(h)].astype(jnp.float32)
        for step in range(count - 1):
            summed = summed + arrived[at, step].astype(jnp.float32)
        total[at] = summed.astype(jnp.bfloat16)
        final = pltpu.make_async_remote_copy(
            src_ref=total.at[at],
            dst_ref=landed.at[at],
            send_sem=t_send.at[at],
            recv_sem=t_recv.at[at],
            device_id={"head": to_head, "video": to_v},
            device_id_type=MESH_ID,
        )

        @pl.when(stays)
        def _(at=at):
            landed[at] = total[at]

        @pl.when(jnp.logical_not(stays))
        def _(final=final):
            final.start()

        finals.append(final)

    @pl.when(jnp.logical_not(stays))
    def _():
        for final in finals:
            final.wait()

    for at in range(chunks):
        out[0, :, at * chunk : (at + 1) * chunk] = landed[at]

    for copy in [rate_out] + i_out + a_out + backs + z_out:
        copy.wait_send()
    for video in videos:
        for at in range(chunks):
            head, copy = part_copy(video, at)

            @pl.when(head != h)
            def _(copy=copy):
                copy.wait_send()


def fused_on_device(
    attention_qkv,
    inner_qkv,
    learn_rate,
    segment_id,
    video_length,
    gate_alpha,
    inner_gain,
    inner_shift,
    first_weight,
    first_bias,
    second_weight,
    second_bias,
    out_weight,
):
    tok = attention_qkv.shape[2]
    width_dev = attention_qkv.shape[3]
    count = lax.axis_size("head")
    ctx_count = lax.axis_size("ctx")
    seq = tok * ctx_count
    slabs = width_dev // LANE // ctx_count
    heads = width_dev // HD
    hidden = first_weight.shape[2]
    columns = out_weight.shape[1]
    chunk = 2 * LANE if columns % (2 * LANE) == 0 else columns
    chunks = columns // chunk
    half = jnp.bfloat16
    full = jnp.float32
    hbm = pl.BlockSpec(memory_space=pl.ANY)
    vmem = pl.BlockSpec(memory_space=pltpu.VMEM)
    smem = pl.BlockSpec(memory_space=pltpu.SMEM)
    dma = pltpu.SemaphoreType.DMA
    return pl.pallas_call(
        fused_kernel,
        out_shape=jax.ShapeDtypeStruct((1, tok, columns), half),
        in_specs=[hbm] * 6 + [vmem, smem] + [vmem] * 5,
        out_specs=vmem,
        scratch_shapes=[
            pltpu.VMEM((slabs, 3, seq, LANE), half),
            pltpu.VMEM((slabs, 3, seq, LANE), half),
            pltpu.VMEM((ctx_count, heads, 1, tok), full),
            pltpu.VMEM((2 * slabs,) + first_weight.shape[1:], half),
            pltpu.VMEM((2 * slabs,) + second_weight.shape[:0:-1], half),
            pltpu.VMEM(out_weight.shape, half),
            pltpu.VMEM((slabs, LANE, hidden), full),
            pltpu.VMEM((slabs, LANE, 2 * hidden), half),
            pltpu.VMEM((slabs, LANE, hidden), full),
            pltpu.VMEM((slabs, LANE, 2 * hidden), half),
            pltpu.VMEM((slabs, 1, 2 * hidden), full),
            pltpu.VMEM((slabs, 1, LANE), full),
            pltpu.VMEM((1, width_dev), full),
            pltpu.VMEM((slabs, 1, LANE), full),
            pltpu.VMEM((slabs, 1, LANE), full),
            pltpu.VMEM((slabs, seq, LANE), full),
            pltpu.VMEM((slabs, seq, LANE), full),
            pltpu.VMEM((seq, seq), full),
            pltpu.VMEM((slabs, seq, LANE), full),
            pltpu.VMEM((slabs, seq, LANE), half),
            pltpu.VMEM((count, 2 * slabs, tok, LANE), half),
            pltpu.VMEM((chunks, count, tok, chunk), half),
            pltpu.VMEM((chunks, count - 1, tok, chunk), half),
            pltpu.VMEM((chunks, tok, chunk), half),
            pltpu.VMEM((chunks, tok, chunk), half),
            dma((2 * slabs + 4,)),
            dma((2 * slabs + 1,)),
            dma((2 * slabs + 1,)),
            dma((slabs,)),
            dma((slabs,)),
            dma((2 * slabs, count - 1)),
            dma((2 * slabs, count - 1)),
            dma((slabs,)),
            dma((chunks, count - 1)),
            dma((chunks, count - 1)),
            dma((chunks,)),
            dma((chunks,)),
            pltpu.SemaphoreType.REGULAR,
            pltpu.SemaphoreType.REGULAR,
        ],
        compiler_params=pltpu.CompilerParams(
            collective_id=0, has_side_effects=True, vmem_limit_bytes=60 * 1024 * 1024
        ),
    )(
        attention_qkv,
        inner_qkv,
        learn_rate.transpose(1, 0, 2),
        first_weight,
        second_weight.transpose(0, 2, 1),
        out_weight,
        segment_id,
        video_length,
        gate_alpha,
        inner_gain,
        inner_shift,
        first_bias,
        second_bias,
    )


def general_on_device(
    attention_qkv,
    inner_qkv,
    learn_rate,
    segment_id,
    video_length,
    gate_alpha,
    inner_gain,
    inner_shift,
    first_weight,
    first_bias,
    second_weight,
    second_bias,
    out_weight,
):
    tok_count = attention_qkv.shape[2]
    width_dev = attention_qkv.shape[3]
    heads_dev = width_dev // HD
    ctx_index = lax.axis_index("ctx")
    ctx_count = lax.axis_size("ctx")
    positions = ctx_index * tok_count + jnp.arange(tok_count, dtype=jnp.int32)
    length_val = video_length[0]
    live_rows = (positions < length_val).astype(jnp.float32)
    kv_pair = attention_qkv[1:, 0]
    kv_wide = with_halo(kv_pair, (("ctx", 1),), tok_count)
    key_pos = (ctx_index - 1) * tok_count + jnp.arange(3 * tok_count, dtype=jnp.int32)
    seg_row = segment_id[0]
    fill_ids = jnp.full((tok_count,), -1, jnp.int32)
    seg_pad = jnp.concatenate([fill_ids, seg_row, fill_ids])
    key_seg = lax.dynamic_slice_in_dim(seg_pad, ctx_index * tok_count, 3 * tok_count, 0)
    query_seg = lax.dynamic_slice_in_dim(seg_row, ctx_index * tok_count, tok_count, 0)
    allowed = (key_seg[None, :] == query_seg[:, None]) & (
        (key_pos[None, :] < length_val) | (key_pos[None, :] == positions[:, None])
    )
    query_heads = attention_qkv[0, 0].reshape(tok_count, heads_dev, HD)
    key_heads = kv_wide[0].reshape(3 * tok_count, heads_dev, HD)
    value_heads = kv_wide[1].reshape(3 * tok_count, heads_dev, HD)
    scores = jnp.einsum(
        "qhd,khd->hqk", query_heads, key_heads, preferred_element_type=jnp.float32
    ) * HD ** (-0.5)
    scores = jnp.where(allowed[None], scores, -1e30)
    row_max = jnp.max(scores, axis=-1, keepdims=True)
    exp_scores = jnp.exp(scores - row_max)
    soft_weights = (exp_scores / jnp.sum(exp_scores, axis=-1, keepdims=True)).astype(jnp.bfloat16)
    attended = jnp.einsum(
        "hqk,khd->qhd", soft_weights, value_heads, preferred_element_type=jnp.float32
    ).reshape(tok_count, width_dev)
    init_state = (
        first_weight.astype(jnp.float32),
        first_bias,
        second_weight.astype(jnp.float32),
        second_bias,
    )
    rate_rows = learn_rate[0] * live_rows[None, :]
    heads_each = -(-heads_dev // ctx_count)
    heads_padded = heads_each * ctx_count
    rows_heads = inner_qkv[:, 0].reshape(3, tok_count, heads_dev, HD)
    rows_padded = jnp.concatenate(
        [rows_heads, jnp.zeros((3, tok_count, heads_padded - heads_dev, HD), rows_heads.dtype)],
        axis=2,
    )
    rates_padded = pad_heads(rate_rows, heads_padded, 0.0)
    whole_rows = lax.all_to_all(rows_padded, "ctx", split_axis=2, concat_axis=1, tiled=True)
    whole_rates = lax.all_to_all(rates_padded, "ctx", split_axis=0, concat_axis=1, tiled=True)
    seq_count = whole_rows.shape[1]
    full_batches = seq_count // MB
    local_qkv = (
        whole_rows.astype(jnp.float32)
        .transpose(0, 2, 1, 3)
        .reshape(3, heads_each, full_batches, MB, HD)
    )
    local_rates = whole_rates.reshape(heads_each, full_batches, MB)
    first_head = ctx_index * heads_each
    local_gain = lax.dynamic_slice_in_dim(
        pad_heads(inner_gain, heads_padded, 1.0), first_head, heads_each, 0
    )
    local_shift = lax.dynamic_slice_in_dim(
        pad_heads(inner_shift, heads_padded, 0.0), first_head, heads_each, 0
    )
    local_state = tuple(
        (
            lax.dynamic_slice_in_dim(
                pad_heads(piece_arr, heads_padded, 0.0), first_head, heads_each, 0
            )
            for piece_arr in init_state
        )
    )
    unused_final, saved_local = jax.vmap(partial(chain_scan, True))(
        local_state, local_qkv[0], local_qkv[1], local_qkv[2], local_rates, local_gain, local_shift
    )
    out_rows = saved_local.reshape(heads_each, seq_count, HD).transpose(1, 0, 2)
    back_rows = lax.all_to_all(
        out_rows.astype(jnp.bfloat16), "ctx", split_axis=0, concat_axis=1, tiled=True
    ).astype(out_rows.dtype)
    inner_flat = back_rows[:, :heads_dev].reshape(tok_count, width_dev)
    combined = ((attended + jnp.tanh(gate_alpha) * inner_flat) * live_rows[:, None]).astype(
        jnp.bfloat16
    )
    terms = jnp.dot(
        combined,
        lax.all_gather(out_weight, "video", axis=1, tiled=True),
        preferred_element_type=jnp.float32,
    )
    mixed = lax.psum_scatter(terms.astype(jnp.bfloat16), "head", scatter_dimension=1, tiled=True)
    return mixed[None]


def solution(mesh):
    placed = (
        P(None, "video", "ctx", "head"),
        P(None, "video", "ctx", "head"),
        P("video", "head", "ctx"),
        P("video", None),
        P("video"),
        P("head"),
        P("head", None),
        P("head", None),
        P("head", None, None),
        P("head", None),
        P("head", None, None),
        P("head", None),
        P("head", "video"),
    )
    shape = mesh.shape
    fused = shape["ctx"] == 2 and shape["head"] == shape["video"] and shape["head"] % 2 == 0

    def on_device(*args):
        heads_dev = args[0].shape[3] // HD
        if fused and heads_dev % (2 * shape["ctx"]) == 0 and args[0].shape[2] % 128 == 0:
            return fused_on_device(*args)
        return general_on_device(*args)

    return jax.shard_map(
        on_device, mesh=mesh, in_specs=placed, out_specs=P("video", "ctx", "head"), check_vma=False
    )
```

```python
from functools import partial

import jax
import jax.numpy as jnp
from jax import lax
from jax.experimental import pallas as pl
from jax.experimental.pallas import tpu as pltpu
from jax.sharding import PartitionSpec as P

HD = 64
MB = 64


gelu_scale = 0.7978845608028654
gelu_cubic = 0.044715


def with_halo(cells, sides, width):
    for axis, dim in sides:
        count = lax.axis_size(axis)
        ends = count - 1
        head = lax.slice_in_dim(cells, 0, width, axis=dim)
        tail = lax.slice_in_dim(cells, cells.shape[dim] - width, cells.shape[dim], axis=dim)
        cells = jnp.concatenate(
            [
                lax.ppermute(tail, axis, [(i, (i + 1) % count) for i in range(ends)]),
                cells,
                lax.ppermute(head, axis, [((i + 1) % count, i) for i in range(ends)]),
            ],
            axis=dim,
        )
    return cells


def matmul_high(first_op, second_op):
    return jnp.matmul(first_op, second_op, precision=lax.Precision.HIGHEST)


def gelu_pair(entries):
    inner_arg = gelu_scale * (entries + gelu_cubic * entries * entries * entries)
    tanh_val = jnp.tanh(inner_arg)
    act_val = 0.5 * entries * (1.0 + tanh_val)
    slope_val = 0.5 * (1.0 + tanh_val) + 0.5 * entries * (
        1.0 - tanh_val * tanh_val
    ) * gelu_scale * (1.0 + 3.0 * gelu_cubic * entries * entries)
    return (act_val, slope_val)


def layer_stats(summed):
    center = summed - jnp.mean(summed, axis=-1, keepdims=True)
    variance = jnp.mean(center * center, axis=-1, keepdims=True)
    inv_std = lax.rsqrt(variance + 1e-06)
    return (center * inv_std, inv_std)


def lower_mask(row_count):
    row_ids = lax.broadcasted_iota(jnp.int32, (row_count, row_count), 0)
    col_ids = lax.broadcasted_iota(jnp.int32, (row_count, row_count), 1)
    return (row_ids >= col_ids).astype(jnp.float32)


def inner_update(inner_state, key_mb, value_mb, rate_mb, norm_gain, norm_shift):
    weight_one, bias_one, weight_two, bias_two = inner_state
    hidden_pre = matmul_high(key_mb, weight_one) + bias_one
    hidden_act, hidden_slope = gelu_pair(hidden_pre)
    output_pre = matmul_high(hidden_act, weight_two) + bias_two
    normed, inv_std = layer_stats(output_pre)
    residual_err = norm_gain * normed + norm_shift - (value_mb - key_mb)
    scaled_err = residual_err * norm_gain
    grad_two = inv_std * (
        scaled_err
        - jnp.mean(scaled_err, axis=-1, keepdims=True)
        - normed * jnp.mean(scaled_err * normed, axis=-1, keepdims=True)
    )
    grad_one = matmul_high(grad_two, weight_two.T) * hidden_slope
    grad_one = grad_one * rate_mb[:, None]
    grad_two = grad_two * rate_mb[:, None]
    new_state = (
        weight_one - matmul_high(key_mb.T, grad_one),
        bias_one - jnp.sum(grad_one, axis=0),
        weight_two - matmul_high(hidden_act.T, grad_two),
        bias_two - jnp.sum(grad_two, axis=0),
    )
    return ((grad_one, hidden_act, grad_two), new_state)


def query_side(inner_state, query_mb, key_mb, grad_pack, norm_gain, norm_shift):
    weight_one, bias_one, weight_two, bias_two = inner_state
    grad_one, hidden_act, grad_two = grad_pack
    causal = lower_mask(query_mb.shape[0])
    first_kernel = (matmul_high(query_mb, key_mb.T) + 1.0) * causal
    query_pre = matmul_high(query_mb, weight_one) + bias_one - matmul_high(first_kernel, grad_one)
    query_act, unused_slope = gelu_pair(query_pre)
    second_kernel = (matmul_high(query_act, hidden_act.T) + 1.0) * causal
    query_out = matmul_high(query_act, weight_two) + bias_two - matmul_high(second_kernel, grad_two)
    normed, unused_inv = layer_stats(query_out)
    return query_mb + norm_gain * normed + norm_shift


def chain_scan(
    keep_queries, inner_state, queries, key_rows, values, rate_vals, norm_gain, norm_shift
):

    def stepper(loop_state, inputs):
        query_mb, key_mb, value_mb, rate_mb = inputs
        grad_pack, new_state = inner_update(
            loop_state, key_mb, value_mb, rate_mb, norm_gain, norm_shift
        )
        return (
            new_state,
            query_side(loop_state, query_mb, key_mb, grad_pack, norm_gain, norm_shift),
        )

    return lax.scan(stepper, inner_state, (queries, key_rows, values, rate_vals))


def pad_heads(array_in, total_heads, fill_value):
    extra = total_heads - array_in.shape[0]
    filler = jnp.full((extra,) + array_in.shape[1:], fill_value, array_in.dtype)
    return jnp.concatenate([array_in, filler], axis=0)


LANE = 128
MESH_ID = pl.DeviceIdType.MESH


def dot_nn(left, right):
    return lax.dot_general(
        left, right, (((1,), (0,)), ((), ())), preferred_element_type=jnp.float32
    )


def dot_nt(left, right):
    return lax.dot_general(
        left, right, (((1,), (1,)), ((), ())), preferred_element_type=jnp.float32
    )


def dot_tn(left, right):
    return lax.dot_general(
        left, right, (((0,), (0,)), ((), ())), preferred_element_type=jnp.float32
    )


def gelu_only(entries):
    inner_arg = gelu_scale * (entries + gelu_cubic * entries * entries * entries)
    return 0.5 * entries * (1.0 + jnp.tanh(inner_arg))


def half_mean(cells, left):
    first = jnp.sum(jnp.where(left, cells, 0.0), axis=-1, keepdims=True)
    second = jnp.sum(jnp.where(left, 0.0, cells), axis=-1, keepdims=True)
    return jnp.where(left, first, second) * (1.0 / HD)


def half_stats(summed, left):
    center = summed - half_mean(summed, left)
    inv_std = lax.rsqrt(half_mean(center * center, left) + 1e-06)
    return (center * inv_std, inv_std)


def split_heads(cells, left):
    wide = cells.astype(jnp.float32)
    return jnp.concatenate(
        [jnp.where(left, wide, 0.0), jnp.where(left, 0.0, wide)], axis=0
    ).astype(cells.dtype)


def fused_kernel(
    aqkv,
    iqkv,
    rate,
    first_w,
    second_w,
    out_w,
    seg,
    length,
    gate,
    gain,
    shift,
    first_b,
    second_b,
    out,
    a_rows,
    i_rows,
    rates,
    fw,
    sw,
    ow,
    w1m,
    w1b,
    w2m,
    w2b,
    b1,
    b2,
    gate_s,
    gain_s,
    shift_s,
    rate_a,
    rate_b,
    bias,
    inner,
    comb,
    gathered,
    parts,
    arrived,
    total,
    landed,
    load_sem,
    y_send,
    y_recv,
    back_send,
    back_recv,
    z_send,
    z_recv,
    own_sem,
    r_send,
    r_recv,
    t_send,
    t_recv,
    low_sem,
    high_sem,
):
    slabs, _, seq, _ = a_rows.shape
    tok = aqkv.shape[2]
    hidden = first_b.shape[1]
    count = lax.axis_size("head")
    c = lax.axis_index("ctx")
    h = lax.axis_index("head")
    v = lax.axis_index("video")
    other = 1 - c
    mine = pl.multiple_of(c * tok, tok)
    theirs = pl.multiple_of(other * tok, tok)
    pairs_heads = 2 * slabs

    def columns(owner, slab):
        return pl.ds(pl.multiple_of((owner * slabs + slab) * LANE, LANE), LANE)

    loads = []
    for slab in range(slabs):
        loads.append(
            pltpu.make_async_copy(
                iqkv.at[:, 0, :, columns(c, slab)],
                i_rows.at[slab, :, pl.ds(mine, tok), :],
                load_sem.at[slab],
            )
        )
    loads.append(pltpu.make_async_copy(rate, rates.at[c], load_sem.at[2 * slabs]))
    loads.append(
        pltpu.make_async_copy(
            first_w.at[pl.ds(c * pairs_heads, pairs_heads)], fw, load_sem.at[2 * slabs + 1]
        )
    )
    loads.append(
        pltpu.make_async_copy(
            second_w.at[pl.ds(c * pairs_heads, pairs_heads)], sw, load_sem.at[2 * slabs + 2]
        )
    )
    a_loads = [
        pltpu.make_async_copy(
            aqkv.at[:, 0, :, columns(c, slab)],
            a_rows.at[slab, :, pl.ds(mine, tok), :],
            load_sem.at[slabs + slab],
        )
        for slab in range(slabs)
    ]
    ow_load = pltpu.make_async_copy(out_w, ow, load_sem.at[2 * slabs + 3])
    for copy in loads + a_loads + [ow_load]:
        copy.start()

    barrier = pltpu.get_barrier_semaphore()
    pl.semaphore_signal(
        barrier, inc=1, device_id={"ctx": other}, device_id_type=MESH_ID
    )
    below, above = v > 0, v < count - 1
    for step in range(1, count):
        pl.semaphore_signal(
            barrier,
            inc=1,
            device_id={"head": lax.rem(h + step, count)},
            device_id_type=MESH_ID,
        )

    def tell(semaphore, inside, video):
        @pl.when(inside)
        def _():
            pl.semaphore_signal(
                semaphore, inc=1, device_id={"video": video}, device_id_type=MESH_ID
            )

    tell(barrier, below, v - 1)
    tell(barrier, above, v + 1)
    pl.semaphore_wait(barrier, count + (v + count - 1) // count + (2 * count - 2 - v) // count)

    def to_partner(src, dst, send, recv):
        return pltpu.make_async_remote_copy(
            src_ref=src,
            dst_ref=dst,
            send_sem=send,
            recv_sem=recv,
            device_id={"ctx": other},
            device_id_type=MESH_ID,
        )

    rate_out = to_partner(
        rate, rates.at[c], y_send.at[2 * slabs], y_recv.at[2 * slabs]
    )
    rate_out.start()
    i_out = [
        to_partner(
            iqkv.at[:, 0, :, columns(other, slab)],
            i_rows.at[slab, :, pl.ds(mine, tok), :],
            y_send.at[slab],
            y_recv.at[slab],
        )
        for slab in range(slabs)
    ]
    a_out = [
        to_partner(
            aqkv.at[:, 0, :, columns(other, slab)],
            a_rows.at[slab, :, pl.ds(mine, tok), :],
            y_send.at[slabs + slab],
            y_recv.at[slabs + slab],
        )
        for slab in range(slabs)
    ]
    for first, second in zip(i_out, a_out):
        first.start()
        second.start()

    for semaphore, first, video, last in (
        (low_sem, below, v + 1, above),
        (high_sem, above, v - 1, below),
    ):

        @pl.when(first)
        def _(semaphore=semaphore):
            pl.semaphore_wait(semaphore, 1)

        tell(semaphore, last, video)

    seq_ids = lax.broadcasted_iota(jnp.int32, (seq, seq), 1)
    row_ids = lax.broadcasted_iota(jnp.int32, (seq, seq), 0)
    len_val = length[0]
    segs = jnp.broadcast_to(seg[...].astype(jnp.float32), (seq, seq))
    allowed = (segs == segs.T) & ((seq_ids < len_val) | (seq_ids == row_ids))
    bias[...] = jnp.where(allowed, 0.0, -1e30)
    live = (lax.broadcasted_iota(jnp.int32, (seq, LANE), 0) < len_val).astype(jnp.float32)
    left = lax.broadcasted_iota(jnp.int32, (MB, LANE), 1) < HD
    left_seq = lax.broadcasted_iota(jnp.int32, (seq, LANE), 1) < HD
    tri = lax.broadcasted_iota(jnp.int32, (MB, MB), 0) >= lax.broadcasted_iota(
        jnp.int32, (MB, MB), 1
    )
    tri = tri.astype(jnp.float32)
    tri_pair = jnp.concatenate([tri, tri], axis=0)

    gate_s[...] = jnp.tanh(gate[...].reshape(1, gate.shape[0]))

    for copy in loads:
        copy.wait()

    def pair_row(ref, head):
        return jnp.concatenate([ref[pl.ds(head, 1), :], ref[pl.ds(head + 1, 1), :]], axis=1)

    for slab in range(slabs):
        head = c * pairs_heads + 2 * slab
        gain_s[slab] = pair_row(gain, head)
        shift_s[slab] = pair_row(shift, head)
        b1[slab] = pair_row(first_b, head)
        b2[slab] = pair_row(second_b, head)
        for raw, kept, used in ((fw, w1m, w1b), (sw, w2m, w2b)):
            upper, lower = raw[2 * slab], raw[2 * slab + 1]
            kept[slab, 0:HD] = upper.astype(jnp.float32)
            kept[slab, HD:LANE] = lower.astype(jnp.float32)
            used[slab] = jnp.zeros_like(used[slab])
            used[slab, 0:HD, 0:hidden] = upper
            used[slab, HD:LANE, hidden : 2 * hidden] = lower

    rate_out.wait_recv()
    for slab in range(slabs):
        head = c * pairs_heads + 2 * slab
        for part in range(seq // tok):
            rows = slice(part * tok, (part + 1) * tok)
            for ahead, store in ((0, rate_a), (1, rate_b)):
                row = rates[part, head + ahead]
                store[slab, rows] = jnp.broadcast_to(row, (LANE, tok)).T * live[rows]

    def inner_step(slab, row):
        rows = pl.ds(row, MB)
        query, key, value = (i_rows[slab, kind, rows, :] for kind in range(3))
        query_f = query.astype(jnp.float32)
        key_f = key.astype(jnp.float32)
        value_f = value.astype(jnp.float32)
        norm_gain = gain_s[slab]
        norm_shift = shift_s[slab]
        weight_one = w1b[slab]
        weight_two = w2b[slab]
        bias_one = b1[slab]
        bias_two = b2[slab]
        pre = dot_nn(jnp.concatenate([key, query], axis=0), weight_one) + bias_one
        hidden_act, slope = gelu_pair(pre[:MB])
        hidden_b = hidden_act.astype(jnp.bfloat16)
        normed, inv_std = half_stats(dot_nt(hidden_b, weight_two) + bias_two, left)
        scaled = (norm_gain * normed + norm_shift - (value_f - key_f)) * norm_gain
        grad_two = inv_std * (
            scaled - half_mean(scaled, left) - normed * half_mean(scaled * normed, left)
        )
        e_a = rate_a[slab, rows, :]
        e_b = rate_b[slab, rows, :]
        wide = [e_a] * (hidden // LANE) + [e_b] * (hidden // LANE)
        grad_one = dot_nn(grad_two.astype(jnp.bfloat16), weight_two) * slope
        grad_one = grad_one * jnp.concatenate(wide, axis=1)
        grad_two = grad_two * jnp.where(left, e_a, e_b)
        one_b = grad_one.astype(jnp.bfloat16)
        two_b = grad_two.astype(jnp.bfloat16)

        first_kernel = (dot_nt(split_heads(query, left), key) + 1.0) * tri_pair
        first_kernel = first_kernel.astype(jnp.bfloat16)
        fix = jnp.concatenate(
            [
                dot_nn(first_kernel[:MB], one_b[:, :hidden]),
                dot_nn(first_kernel[MB:], one_b[:, hidden:]),
            ],
            axis=1,
        )
        query_act = gelu_only(pre[MB:] - fix).astype(jnp.bfloat16)
        second_kernel = jnp.concatenate(
            [
                dot_nt(query_act[:, :hidden], hidden_b[:, :hidden]),
                dot_nt(query_act[:, hidden:], hidden_b[:, hidden:]),
            ],
            axis=0,
        )
        second_kernel = ((second_kernel + 1.0) * tri_pair).astype(jnp.bfloat16)
        fix_two = dot_nn(second_kernel, two_b)
        fix_two = jnp.where(left, fix_two[:MB], fix_two[MB:])
        query_out = dot_nt(query_act, weight_two) + bias_two - fix_two
        normed_out, _ = half_stats(query_out, left)
        inner[slab, rows, :] = query_f + norm_gain * normed_out + norm_shift

        for kept, used, change in (
            (w1m, w1b, dot_tn(key, one_b)),
            (w2m, w2b, dot_tn(two_b, hidden_b)),
        ):
            upper = kept[slab, 0:HD] - change[:HD, :hidden]
            lower = kept[slab, HD:LANE] - change[HD:, hidden:]
            kept[slab, 0:HD] = upper
            kept[slab, HD:LANE] = lower
            used[slab, 0:HD, 0:hidden] = upper.astype(jnp.bfloat16)
            used[slab, HD:LANE, hidden : 2 * hidden] = lower.astype(jnp.bfloat16)
        b1[slab] = bias_one - jnp.sum(grad_one, axis=0, keepdims=True)
        b2[slab] = bias_two - jnp.sum(grad_two, axis=0, keepdims=True)

    def to_video(src, video, spot, step):
        return pltpu.make_async_remote_copy(
            src_ref=src,
            dst_ref=gathered.at[v, spot],
            send_sem=z_send.at[spot, step - 1],
            recv_sem=z_recv.at[spot, step - 1],
            device_id={"video": video},
            device_id_type=MESH_ID,
        )

    def spread(src, spot):
        copies = []
        for step in range(count - 1, 0, -1):
            copy = to_video(src, lax.rem(v + step, count), spot, step)
            copy.start()
            copies.append(copy)
        return copies

    z_out = []
    backs = []
    owns = []
    for slab in range(slabs):
        i_out[slab].wait_recv()

        def batch_step(batch, carry, slab=slab):
            inner_step(slab, pl.multiple_of(batch * MB, MB))
            return carry

        lax.fori_loop(0, seq // MB, batch_step, 0, unroll=True)
        a_loads[slab].wait()
        a_out[slab].wait_recv()
        query, key, value = (a_rows[slab, kind] for kind in range(3))
        scores = dot_nt(split_heads(query, left_seq), key) * HD ** (-0.5)
        halves = []
        for part in range(2):
            mine_scores = scores[part * seq : (part + 1) * seq] + bias[...]
            top = jnp.max(mine_scores, axis=-1, keepdims=True)
            weights = jnp.exp(mine_scores - top)
            mass = jnp.sum(weights, axis=-1, keepdims=True)
            halves.append(dot_nn(weights.astype(jnp.bfloat16), value) / mass)
        attended = jnp.where(left_seq, halves[0], halves[1])
        gate_row = gate_s[:, columns(c, slab)]
        comb[slab] = ((attended + gate_row * inner[slab]) * live).astype(jnp.bfloat16)
        spot = c * slabs + slab
        back = to_partner(
            comb.at[slab, pl.ds(theirs, tok), :],
            gathered.at[v, spot],
            back_send.at[slab],
            back_recv.at[slab],
        )
        back.start()
        backs.append(back)
        own = pltpu.make_async_copy(
            comb.at[slab, pl.ds(mine, tok), :], gathered.at[v, spot], own_sem.at[slab]
        )
        own.start()
        owns.append(own)
        z_out += spread(comb.at[slab, pl.ds(mine, tok), :], spot)
        if slab:
            backs[slab - 1].wait_recv()
            far = other * slabs + slab - 1
            z_out += spread(gathered.at[v, far], far)
    backs[slabs - 1].wait_recv()
    far = other * slabs + slabs - 1
    z_out += spread(gathered.at[v, far], far)
    for own in owns:
        own.wait()
    ow_load.wait()

    def owner_of(video):
        return lax.rem(video, 2) * (count // 2) + video // 2

    def video_of(head):
        return lax.rem(head, count // 2) * 2 + head // (count // 2)

    chunks, _, _, chunk = parts.shape
    toward = 1 - 2 * (v // (count // 2))

    def part_copy(video, at):
        head = owner_of(video)
        ahead = lax.rem(head - h + count, count)
        slot = lax.rem(ahead + count - 1, count)
        return head, pltpu.make_async_remote_copy(
            src_ref=parts.at[at, video],
            dst_ref=arrived.at[at, slot],
            send_sem=r_send.at[at, slot],
            recv_sem=r_recv.at[at, slot],
            device_id={"head": head},
            device_id_type=MESH_ID,
        )

    videos = []
    for near in range(count):
        video = lax.rem(v + toward * near + count, count)
        videos.append(video)
        if near:
            step = lax.rem(v - video + count, count)
            for spot in range(2 * slabs):
                pltpu.make_async_remote_copy(
                    src_ref=gathered.at[video, spot],
                    dst_ref=gathered.at[video, spot],
                    send_sem=z_send.at[spot, step - 1],
                    recv_sem=z_recv.at[spot, step - 1],
                    device_id={"video": video},
                    device_id_type=MESH_ID,
                ).wait_recv()
        rows_video = jnp.concatenate(
            [gathered[video, spot] for spot in range(2 * slabs)], axis=1
        )
        for at in range(chunks):
            piece = dot_nn(rows_video, ow[:, at * chunk : (at + 1) * chunk])
            parts[at, video] = piece.astype(jnp.bfloat16)
            head, copy = part_copy(video, at)

            @pl.when(head != h)
            def _(copy=copy):
                copy.start()

    to_head, to_v = v, video_of(h)
    stays = (to_head == h) & (to_v == v)
    finals = []
    for at in range(chunks):
        for step in range(1, count):
            pltpu.make_async_remote_copy(
                src_ref=arrived.at[at, step - 1],
                dst_ref=arrived.at[at, step - 1],
                send_sem=r_send.at[at, step - 1],
                recv_sem=r_recv.at[at, step - 1],
                device_id={"head": lax.rem(h + step, count)},
                device_id_type=MESH_ID,
            ).wait_recv()
        summed = parts[at, video_of(h)].astype(jnp.float32)
        for step in range(count - 1):
            summed = summed + arrived[at, step].astype(jnp.float32)
        total[at] = summed.astype(jnp.bfloat16)
        final = pltpu.make_async_remote_copy(
            src_ref=total.at[at],
            dst_ref=landed.at[at],
            send_sem=t_send.at[at],
            recv_sem=t_recv.at[at],
            device_id={"head": to_head, "video": to_v},
            device_id_type=MESH_ID,
        )

        @pl.when(stays)
        def _(at=at):
            landed[at] = total[at]

        @pl.when(jnp.logical_not(stays))
        def _(final=final):
            final.start()

        finals.append(final)

    @pl.when(jnp.logical_not(stays))
    def _():
        for final in finals:
            final.wait()

    for at in range(chunks):
        out[0, :, at * chunk : (at + 1) * chunk] = landed[at]

    for copy in [rate_out] + i_out + a_out + backs + z_out:
        copy.wait_send()
    for video in videos:
        for at in range(chunks):
            head, copy = part_copy(video, at)

            @pl.when(head != h)
            def _(copy=copy):
                copy.wait_send()


def fused_on_device(
    attention_qkv,
    inner_qkv,
    learn_rate,
    segment_id,
    video_length,
    gate_alpha,
    inner_gain,
    inner_shift,
    first_weight,
    first_bias,
    second_weight,
    second_bias,
    out_weight,
):
    tok = attention_qkv.shape[2]
    width_dev = attention_qkv.shape[3]
    count = lax.axis_size("head")
    ctx_count = lax.axis_size("ctx")
    seq = tok * ctx_count
    slabs = width_dev // LANE // ctx_count
    heads = width_dev // HD
    hidden = first_weight.shape[2]
    columns = out_weight.shape[1]
    chunk = 2 * LANE if columns % (2 * LANE) == 0 else columns
    chunks = columns // chunk
    half = jnp.bfloat16
    full = jnp.float32
    hbm = pl.BlockSpec(memory_space=pl.ANY)
    vmem = pl.BlockSpec(memory_space=pltpu.VMEM)
    smem = pl.BlockSpec(memory_space=pltpu.SMEM)
    dma = pltpu.SemaphoreType.DMA
    return pl.pallas_call(
        fused_kernel,
        out_shape=jax.ShapeDtypeStruct((1, tok, columns), half),
        in_specs=[hbm] * 6 + [vmem, smem] + [vmem] * 5,
        out_specs=vmem,
        scratch_shapes=[
            pltpu.VMEM((slabs, 3, seq, LANE), half),
            pltpu.VMEM((slabs, 3, seq, LANE), half),
            pltpu.VMEM((ctx_count, heads, 1, tok), full),
            pltpu.VMEM((2 * slabs,) + first_weight.shape[1:], half),
            pltpu.VMEM((2 * slabs,) + second_weight.shape[:0:-1], half),
            pltpu.VMEM(out_weight.shape, half),
            pltpu.VMEM((slabs, LANE, hidden), full),
            pltpu.VMEM((slabs, LANE, 2 * hidden), half),
            pltpu.VMEM((slabs, LANE, hidden), full),
            pltpu.VMEM((slabs, LANE, 2 * hidden), half),
            pltpu.VMEM((slabs, 1, 2 * hidden), full),
            pltpu.VMEM((slabs, 1, LANE), full),
            pltpu.VMEM((1, width_dev), full),
            pltpu.VMEM((slabs, 1, LANE), full),
            pltpu.VMEM((slabs, 1, LANE), full),
            pltpu.VMEM((slabs, seq, LANE), full),
            pltpu.VMEM((slabs, seq, LANE), full),
            pltpu.VMEM((seq, seq), full),
            pltpu.VMEM((slabs, seq, LANE), full),
            pltpu.VMEM((slabs, seq, LANE), half),
            pltpu.VMEM((count, 2 * slabs, tok, LANE), half),
            pltpu.VMEM((chunks, count, tok, chunk), half),
            pltpu.VMEM((chunks, count - 1, tok, chunk), half),
            pltpu.VMEM((chunks, tok, chunk), half),
            pltpu.VMEM((chunks, tok, chunk), half),
            dma((2 * slabs + 4,)),
            dma((2 * slabs + 1,)),
            dma((2 * slabs + 1,)),
            dma((slabs,)),
            dma((slabs,)),
            dma((2 * slabs, count - 1)),
            dma((2 * slabs, count - 1)),
            dma((slabs,)),
            dma((chunks, count - 1)),
            dma((chunks, count - 1)),
            dma((chunks,)),
            dma((chunks,)),
            pltpu.SemaphoreType.REGULAR,
            pltpu.SemaphoreType.REGULAR,
        ],
        compiler_params=pltpu.CompilerParams(
            collective_id=0, has_side_effects=True, vmem_limit_bytes=60 * 1024 * 1024
        ),
    )(
        attention_qkv,
        inner_qkv,
        learn_rate.transpose(1, 0, 2),
        first_weight,
        second_weight.transpose(0, 2, 1),
        out_weight,
        segment_id,
        video_length,
        gate_alpha,
        inner_gain,
        inner_shift,
        first_bias,
        second_bias,
    )


def general_on_device(
    attention_qkv,
    inner_qkv,
    learn_rate,
    segment_id,
    video_length,
    gate_alpha,
    inner_gain,
    inner_shift,
    first_weight,
    first_bias,
    second_weight,
    second_bias,
    out_weight,
):
    tok_count = attention_qkv.shape[2]
    width_dev = attention_qkv.shape[3]
    heads_dev = width_dev // HD
    ctx_index = lax.axis_index("ctx")
    ctx_count = lax.axis_size("ctx")
    positions = ctx_index * tok_count + jnp.arange(tok_count, dtype=jnp.int32)
    length_val = video_length[0]
    live_rows = (positions < length_val).astype(jnp.float32)
    kv_pair = attention_qkv[1:, 0]
    kv_wide = with_halo(kv_pair, (("ctx", 1),), tok_count)
    key_pos = (ctx_index - 1) * tok_count + jnp.arange(3 * tok_count, dtype=jnp.int32)
    seg_row = segment_id[0]
    fill_ids = jnp.full((tok_count,), -1, jnp.int32)
    seg_pad = jnp.concatenate([fill_ids, seg_row, fill_ids])
    key_seg = lax.dynamic_slice_in_dim(seg_pad, ctx_index * tok_count, 3 * tok_count, 0)
    query_seg = lax.dynamic_slice_in_dim(seg_row, ctx_index * tok_count, tok_count, 0)
    allowed = (key_seg[None, :] == query_seg[:, None]) & (
        (key_pos[None, :] < length_val) | (key_pos[None, :] == positions[:, None])
    )
    query_heads = attention_qkv[0, 0].reshape(tok_count, heads_dev, HD)
    key_heads = kv_wide[0].reshape(3 * tok_count, heads_dev, HD)
    value_heads = kv_wide[1].reshape(3 * tok_count, heads_dev, HD)
    scores = jnp.einsum(
        "qhd,khd->hqk", query_heads, key_heads, preferred_element_type=jnp.float32
    ) * HD ** (-0.5)
    scores = jnp.where(allowed[None], scores, -1e30)
    row_max = jnp.max(scores, axis=-1, keepdims=True)
    exp_scores = jnp.exp(scores - row_max)
    soft_weights = (exp_scores / jnp.sum(exp_scores, axis=-1, keepdims=True)).astype(jnp.bfloat16)
    attended = jnp.einsum(
        "hqk,khd->qhd", soft_weights, value_heads, preferred_element_type=jnp.float32
    ).reshape(tok_count, width_dev)
    init_state = (
        first_weight.astype(jnp.float32),
        first_bias,
        second_weight.astype(jnp.float32),
        second_bias,
    )
    rate_rows = learn_rate[0] * live_rows[None, :]
    heads_each = -(-heads_dev // ctx_count)
    heads_padded = heads_each * ctx_count
    rows_heads = inner_qkv[:, 0].reshape(3, tok_count, heads_dev, HD)
    rows_padded = jnp.concatenate(
        [rows_heads, jnp.zeros((3, tok_count, heads_padded - heads_dev, HD), rows_heads.dtype)],
        axis=2,
    )
    rates_padded = pad_heads(rate_rows, heads_padded, 0.0)
    whole_rows = lax.all_to_all(rows_padded, "ctx", split_axis=2, concat_axis=1, tiled=True)
    whole_rates = lax.all_to_all(rates_padded, "ctx", split_axis=0, concat_axis=1, tiled=True)
    seq_count = whole_rows.shape[1]
    full_batches = seq_count // MB
    local_qkv = (
        whole_rows.astype(jnp.float32)
        .transpose(0, 2, 1, 3)
        .reshape(3, heads_each, full_batches, MB, HD)
    )
    local_rates = whole_rates.reshape(heads_each, full_batches, MB)
    first_head = ctx_index * heads_each
    local_gain = lax.dynamic_slice_in_dim(
        pad_heads(inner_gain, heads_padded, 1.0), first_head, heads_each, 0
    )
    local_shift = lax.dynamic_slice_in_dim(
        pad_heads(inner_shift, heads_padded, 0.0), first_head, heads_each, 0
    )
    local_state = tuple(
        (
            lax.dynamic_slice_in_dim(
                pad_heads(piece_arr, heads_padded, 0.0), first_head, heads_each, 0
            )
            for piece_arr in init_state
        )
    )
    unused_final, saved_local = jax.vmap(partial(chain_scan, True))(
        local_state, local_qkv[0], local_qkv[1], local_qkv[2], local_rates, local_gain, local_shift
    )
    out_rows = saved_local.reshape(heads_each, seq_count, HD).transpose(1, 0, 2)
    back_rows = lax.all_to_all(
        out_rows.astype(jnp.bfloat16), "ctx", split_axis=0, concat_axis=1, tiled=True
    ).astype(out_rows.dtype)
    inner_flat = back_rows[:, :heads_dev].reshape(tok_count, width_dev)
    combined = ((attended + jnp.tanh(gate_alpha) * inner_flat) * live_rows[:, None]).astype(
        jnp.bfloat16
    )
    terms = jnp.dot(
        combined,
        lax.all_gather(out_weight, "video", axis=1, tiled=True),
        preferred_element_type=jnp.float32,
    )
    mixed = lax.psum_scatter(terms.astype(jnp.bfloat16), "head", scatter_dimension=1, tiled=True)
    return mixed[None]


def solution(mesh):
    placed = (
        P(None, "video", "ctx", "head"),
        P(None, "video", "ctx", "head"),
        P("video", "head", "ctx"),
        P("video", None),
        P("video"),
        P("head"),
        P("head", None),
        P("head", None),
        P("head", None, None),
        P("head", None),
        P("head", None, None),
        P("head", None),
        P("head", "video"),
    )
    shape = mesh.shape
    fused = shape["ctx"] == 2 and shape["head"] == shape["video"] and shape["head"] % 2 == 0

    def on_device(*args):
        heads_dev = args[0].shape[3] // HD
        if fused and heads_dev % (2 * shape["ctx"]) == 0 and args[0].shape[2] % 128 == 0:
            return fused_on_device(*args)
        return general_on_device(*args)

    return jax.shard_map(
        on_device, mesh=mesh, in_specs=placed, out_specs=P("video", "ctx", "head"), check_vma=False
    )
```
